768 devices in a mesh: pole: 1, prow: 16 (over y, core), pcol: 48 (over z, x).
Axes of the slice: x: 4, y: 8, z: 12, core: 2. Of those that a mesh axis runs over, the one named last changes fastest.
Arguments:
- hamiltonian: bfloat16 [12288, 12288], P(('prow', 'pcol')), may hold values from -2 to 32, as said below
- margin: bfloat16 [12288, 12288], P(('prow', 'pcol')), may hold values from -1 to 1, as said below
- pole_shift: float32 [2], P('pole'), may hold values from 0.3 to 1.5
- row_map: int32 [12288], P('prow'), may hold values from 0 to 12287, as said below
- parent: int32 [96], replicated, may hold values from 1 to 96, as said below
Outputs:
- factored: float32 [2, 12288, 12288], P('pole', 'prow', 'pcol')
The draws below stay inside these ranges and needn't reach their ends.
Inputs may be any that keep to these rules, and one draw needn't show every extreme that they name: For each aligned block of 768 rows, row_map maps the block's rows one to one onto the same block's indices. parent[s] is greater than s; the value 96 marks a root. Supernode 0's parent is 1 and the last supernode is a root. `hamiltonian`: as a matrix over orbitals it is symmetric. `margin`: as a matrix over orbitals it is symmetric, with ones on its diagonal.
All inputs are finite; a program needn't handle non-finite values.
Results may differ from the reference program's by a relative error of at most 0.0023.
Values may be sent and summed in bfloat16 or wider, within the bound.
No kernel may reach another device: no remote copies, remote signals or barrier semaphores. Data moves between devices by JAX's collectives and lax.ppermute only.
A program may use at most 32 MiB of HBM per device.

```python
import jax
import jax.numpy as jnp
from jax import lax

SN = 128
RB = 6
STEPS = 3
NSI = 4
NBW = 96
CB = 2
NO = 12288
N_PROW = 16
N_PCOL = 48


def orbital_order(key):
    base_key = jax.random.fold_in(key, 101)
    span_rows = RB * SN
    groups_count = NO // span_rows
    group_keys = jax.random.split(base_key, groups_count)
    shuffles = jax.vmap(lambda group_key: jax.random.permutation(group_key, span_rows))(group_keys)
    offsets = jnp.arange(groups_count, dtype=jnp.int32) * span_rows
    return (shuffles.astype(jnp.int32) + offsets[:, None]).reshape(NO)


def natural_symmetric(key, intra, inter, diag_lo, diag_hi):
    first_key, second_key = jax.random.split(key)
    noise = jax.random.uniform(first_key, (NO, NO), jnp.float32, -1.0, 1.0)
    mirrored = 0.5 * (noise + noise.T)
    nodes = jnp.arange(NO, dtype=jnp.int32) // SN
    scaled = mirrored * jnp.where(nodes[:, None] == nodes[None, :], intra, inter)
    onsite = jax.random.uniform(second_key, (NO,), jnp.float32, diag_lo, diag_hi)
    positions = jnp.arange(NO, dtype=jnp.int32)
    return jnp.where(positions[:, None] == positions[None, :], onsite[None, :], scaled)


def orbital_layout(key, natural_matrix):
    row_order = orbital_order(key)
    stored_place = jnp.arange(NO, dtype=jnp.int32)
    span_rows = RB * SN
    span_cols = CB * SN
    grid_rows = NBW // RB
    grid_cols = NBW // CB
    row_natural = (stored_place % span_rows // SN * grid_rows + stored_place // span_rows) * SN + stored_place % SN
    col_natural = (stored_place % span_cols // SN * grid_cols + stored_place // span_cols) * SN + stored_place % SN
    orbital_natural = jnp.zeros((NO,), jnp.int32).at[row_order].set(row_natural)
    return natural_matrix[orbital_natural][:, col_natural]


def draw_hamiltonian(key, part):
    return orbital_layout(key, natural_symmetric(jax.random.fold_in(key, 202), 1.3, 0.65, 16.0, 32.0)).astype(jnp.bfloat16)


def draw_margin(key, part):
    return orbital_layout(key, natural_symmetric(jax.random.fold_in(key, 303), 0.25, 0.08, 1.0, 1.0)).astype(jnp.bfloat16)


def draw_row_map(key, part):
    return orbital_order(key)


def draw_parent(key, part):
    node_index = jnp.arange(NBW, dtype=jnp.int32)
    reach_limit = jnp.where(node_index == 0, 1, jnp.minimum(NBW - node_index, 5))
    random_bits = jax.random.randint(jax.random.fold_in(key, 404), (NBW,), 0, 1 << 20, dtype=jnp.int32)
    return (node_index + random_bits % reach_limit + 1).astype(jnp.int32)


def setup_inputs(seed: int = 0, part: int = 0) -> dict:
    splits = jax.random.split(jax.random.key(seed), 6)
    part_keys = jax.random.split(jax.random.fold_in(splits[5], part), 6)
    return {
        "hamiltonian": draw_hamiltonian(jax.random.fold_in(splits[5], 71), part),
        "margin": draw_margin(jax.random.fold_in(splits[5], 71), part),
        "pole_shift": jnp.clip(jax.random.uniform(part_keys[2], (2,), jnp.float32, 0.3, 1.5), 0.3, 1.5),
        "row_map": draw_row_map(jax.random.fold_in(splits[5], 71), part),
        "parent": draw_parent(jax.random.fold_in(splits[5], 71), part),
    }


def complex_product(left_pair, right_pair):
    highest = lax.Precision.HIGHEST
    real_part = jnp.dot(left_pair[0], right_pair[0], precision=highest, preferred_element_type=jnp.float32) - jnp.dot(left_pair[1], right_pair[1], precision=highest, preferred_element_type=jnp.float32)
    imag_part = jnp.dot(left_pair[0], right_pair[1], precision=highest, preferred_element_type=jnp.float32) + jnp.dot(left_pair[1], right_pair[0], precision=highest, preferred_element_type=jnp.float32)
    return jnp.stack([real_part, imag_part])


def structure(parent, node_count):
    node_index = jnp.arange(node_count, dtype=jnp.int32)
    reached = (parent[:, None] == node_index[None, :]).astype(jnp.int32)
    for level_index in range(node_count.bit_length()):
        reached = jnp.minimum(reached + jnp.dot(reached, reached), 1)
    diagonal_ones = (node_index[:, None] == node_index[None, :]).astype(jnp.int32)
    return jnp.minimum(diagonal_ones + reached + reached.T, 1)


def invert_pivot(pivot, sweeps):
    pivot_size = pivot.shape[-1]
    places = jnp.arange(pivot_size, dtype=jnp.int32)
    identity_real = (places[:, None] == places[None, :]).astype(jnp.float32)
    diag_real = jnp.diagonal(pivot[0])
    diag_imag = jnp.diagonal(pivot[1])
    modulus = diag_real * diag_real + diag_imag * diag_imag
    approx = jnp.stack([identity_real * (diag_real / modulus)[None, :], identity_real * (-diag_imag / modulus)[None, :]])
    for sweep_index in range(sweeps):
        product = complex_product(pivot, approx)
        residue = jnp.stack([2.0 * identity_real - product[0], -product[1]])
        approx = complex_product(approx, residue)
    return approx


def reference(hamiltonian, margin, pole_shift, row_map, parent):
    natural = jnp.arange(NO, dtype=jnp.int32)
    supernode = natural // SN
    within = natural % SN
    row_place = ((supernode % N_PROW) * RB + supernode // N_PROW) * SN + within
    col_place = ((supernode % N_PCOL) * CB + supernode // N_PCOL) * SN + within
    ham_rows = hamiltonian[row_map].astype(jnp.float32)
    over_rows = margin[row_map].astype(jnp.float32)
    real_part = (ham_rows - pole_shift[0] * over_rows)[row_place][:, col_place]
    imag_part = (-pole_shift[1] * over_rows)[row_place][:, col_place]
    pattern = structure(parent, NBW)
    pattern_full = jnp.repeat(jnp.repeat(pattern, SN, axis=0), SN, axis=1).astype(jnp.float32)
    matrix = jnp.stack([real_part, imag_part]) * pattern_full[None]
    for elimination in range(STEPS):
        lower_edge = elimination * SN
        upper_edge = lower_edge + SN
        inverse = invert_pivot(matrix[:, lower_edge:upper_edge, lower_edge:upper_edge], NSI)
        factor = complex_product(matrix[:, upper_edge:, lower_edge:upper_edge], inverse)
        update = complex_product(factor, matrix[:, lower_edge:upper_edge, upper_edge:])
        matrix = matrix.at[:, upper_edge:, upper_edge:].add(-update)
        matrix = matrix.at[:, upper_edge:, lower_edge:upper_edge].set(factor)
    stored_place = jnp.arange(NO, dtype=jnp.int32)
    span_rows = RB * SN
    span_cols = CB * SN
    row_natural = (((stored_place % span_rows) // SN) * N_PROW + stored_place // span_rows) * SN + stored_place % SN
    col_natural = (((stored_place % span_cols) // SN) * N_PCOL + stored_place // span_cols) * SN + stored_place % SN
    return matrix[:, row_natural][:, :, col_natural]
```

```python
import functools

import jax
import jax.numpy as jnp
from jax import lax
from jax.experimental import pallas as pl
from jax.experimental.pallas import tpu as pltpu
from jax.sharding import PartitionSpec as P

SN = 128
STEPS = 3
NSI = 4
N_Z = 12
N_X = 4
F32 = jnp.float32
BF16 = jnp.bfloat16


def split(x):
    high = x.astype(BF16)
    return high, (x - high.astype(F32)).astype(BF16)


def mm(left, right):
    left_high, left_low = split(left)
    right_high, right_low = split(right)
    dot = functools.partial(jnp.dot, preferred_element_type=F32)
    return dot(left_high, right_high) + (dot(left_high, right_low) + dot(left_low, right_high))


def embed(column):
    real, imag = column[:SN], column[SN:]
    return jnp.concatenate([column, jnp.concatenate([-imag, real], axis=0)], axis=1)


def times(scalar, column):
    real, imag = column[: column.shape[0] // 2], column[column.shape[0] // 2 :]
    return jnp.concatenate(
        [scalar[0] * real - scalar[1] * imag, scalar[0] * imag + scalar[1] * real], axis=0
    )


def invert_pivot(pivot):
    row = lax.broadcasted_iota(jnp.int32, (SN, SN), 0)
    col = lax.broadcasted_iota(jnp.int32, (SN, SN), 1)
    eye = (row == col).astype(F32)
    real, imag = pivot[:SN], pivot[SN:]
    diag_real = jnp.sum(real * eye, axis=0, keepdims=True)
    diag_imag = jnp.sum(imag * eye, axis=0, keepdims=True)
    modulus = diag_real * diag_real + diag_imag * diag_imag
    inv_real, inv_imag = diag_real / modulus, -diag_imag / modulus
    residue = jnp.concatenate(
        [eye - (real * inv_real - imag * inv_imag), -(real * inv_imag + imag * inv_real)], axis=0
    )
    scale_real = jnp.sum(eye * inv_real, axis=1, keepdims=True)
    scale_imag = jnp.sum(eye * inv_imag, axis=1, keepdims=True)
    plus_real, plus_imag = eye + residue[:SN], residue[SN:]
    approx = jnp.concatenate(
        [
            scale_real * plus_real - scale_imag * plus_imag,
            scale_real * plus_imag + scale_imag * plus_real,
        ],
        axis=0,
    )
    power = mm(embed(residue), residue)
    for sweep in range(NSI - 1):
        if sweep < NSI - 2:
            both = mm(jnp.concatenate([embed(approx), embed(power)], axis=0), power)
            approx = approx + both[: 2 * SN]
            power = both[2 * SN :]
        else:
            approx = approx + mm(embed(approx), power)
    return approx


def permute_kernel(place_ref, mask_ref, raw_ref, out_ref):
    height = raw_ref.shape[0]
    for slot in range(height // SN):
        rows = slice(slot * SN, (slot + 1) * SN)
        pick = (
            place_ref[rows, :] == lax.broadcasted_iota(jnp.int32, (SN, height), 1)
        ).astype(BF16)
        got = jnp.dot(pick, raw_ref[...], preferred_element_type=F32)
        for part in range(2 * STEPS):
            out_ref[rows, part * SN : (part + 1) * SN] = (
                got[:, part * SN : (part + 1) * SN] * mask_ref[slot, part % STEPS]
            ).astype(BF16)


def root_kernel(shift_ref, which_ref, a0_ref, a1_ref, a2_ref, r0_ref, r1_ref, w_ref, u_ref):
    z_real, z_imag = shift_ref[0], shift_ref[1]
    my_col = which_ref[0]

    def block(ref, step, transposed):
        ham = ref[:, step * SN : (step + 1) * SN].astype(F32)
        over = ref[:, (STEPS + step) * SN : (STEPS + step + 1) * SN].astype(F32)
        real, imag = ham - z_real * over, -z_imag * over
        if transposed:
            real, imag = real.T, imag.T
        return jnp.concatenate([real, imag], axis=0)

    a_refs = (a0_ref, a1_ref, a2_ref)
    rows = [
        jnp.concatenate(
            [block(a_refs[t], s, False) for s in range(STEPS)]
            + [block(r0_ref, t, True), block(r1_ref, t, True)],
            axis=1,
        )
        for t in range(STEPS)
    ]
    inverse, solved, lower = [], [], {}
    for t in range(STEPS):
        inverse.append(invert_pivot(rows[t][:, t * SN : (t + 1) * SN]))
        solved.append(mm(embed(inverse[t]), rows[t][:, (t + 1) * SN :]))
        for i in range(t + 1, STEPS):
            lower[i, t] = embed(rows[i][:, t * SN : (t + 1) * SN])
            changed = rows[i][:, (t + 1) * SN :] - mm(lower[i, t], solved[t])
            rows[i] = jnp.concatenate([rows[i][:, : (t + 1) * SN], changed], axis=1)

    def upper(t, s):
        return embed(solved[t][:, (s - t - 1) * SN : (s - t) * SN])

    def right(t):
        return solved[t][:, (STEPS - 1 - t) * SN :]

    def chosen(t, special):
        unit = jnp.where(my_col == t, inverse[t], jnp.zeros_like(inverse[t]))
        first = jnp.where(special, unit, right(t)[:, :SN])
        return jnp.concatenate([first, right(t)[:, SN:]], axis=1)

    y = [chosen(t, my_col < STEPS) for t in range(STEPS)]
    w2 = y[2]
    w1 = y[1] - mm(upper(1, 2), w2)
    w0 = y[0] - (mm(upper(0, 1), w1) + mm(upper(0, 2), w2))
    for t, w in enumerate((w0, w1, w2)):
        w_ref[0, t * SN : (t + 1) * SN, :] = w[:SN].astype(BF16)
        w_ref[1, t * SN : (t + 1) * SN, :] = w[SN:].astype(BF16)
    u1 = mm(lower[1, 0], chosen(0, my_col < 1))
    u2 = mm(lower[2, 0], chosen(0, my_col < 2)) + mm(lower[2, 1], chosen(1, my_col < 2))
    for i, u in enumerate((u1, u2)):
        u_ref[i, 0] = u[:SN].astype(BF16)
        u_ref[i, 1] = u[SN:].astype(BF16)


def final_kernel(
    shift_ref, which_ref, mask_ref, place_ref, main_ref, panel_ref, w_ref, u_ref, out_ref
):
    z_real, z_imag = shift_ref[0], shift_ref[1]
    my_row, my_col, grid_rows = which_ref[1], which_ref[0], which_ref[2]
    height, width = out_ref.shape[1], out_ref.shape[2]
    w_real, w_imag = w_ref[0].astype(F32), w_ref[1].astype(F32)
    depth = w_real.shape[0]
    w_all = jnp.concatenate(
        [
            jnp.concatenate([w_ref[0], w_ref[1]], axis=1),
            jnp.concatenate(
                [z_imag * w_imag - z_real * w_real, -z_real * w_imag - z_imag * w_real], axis=1
            ).astype(BF16),
        ],
        axis=0,
    )
    ham_raw = main_ref[:, :16, :].reshape(height, width)
    over_raw = main_ref[:, 16:, :].reshape(height, width)
    for slot in range(height // SN):
        rows = slice(slot * SN, (slot + 1) * SN)
        pick = (
            place_ref[rows, :] == lax.broadcasted_iota(jnp.int32, (SN, height), 1)
        ).astype(BF16)
        ham = jnp.dot(pick, ham_raw, preferred_element_type=F32)
        over = jnp.dot(pick, over_raw, preferred_element_type=F32)
        real, imag = ham - z_real * over, -z_imag * over
        change = jnp.dot(panel_ref[rows, :], w_all, preferred_element_type=F32)
        change_real, change_imag = change[:, :width], change[:, width:]
        if slot == 0:
            early = my_row < STEPS
            change_real = jnp.where(early, u_ref[0].astype(F32), change_real)
            change_imag = jnp.where(early, u_ref[1].astype(F32), change_imag)
        node = my_row + grid_rows * slot
        for half in range(width // SN):
            cols = slice(half * SN, (half + 1) * SN)
            keep, sign = mask_ref[slot, half], F32(-1.0)
            if half == 0:
                factor = (my_col < STEPS) & (node > my_col)
                keep = jnp.where(factor, 0.0, keep)
                sign = jnp.where(factor, 1.0, -1.0)
            out_ref[0, rows, cols] = real[:, cols] * keep + change_real[:, cols] * sign
            out_ref[1, rows, cols] = imag[:, cols] * keep + change_imag[:, cols] * sign


def structure(parent, node_count):
    node_index = jnp.arange(node_count, dtype=jnp.int32)
    reached = (parent[:, None] == node_index[None, :]).astype(BF16)
    for level_index in range(node_count.bit_length()):
        more = jnp.dot(reached, reached, preferred_element_type=F32)
        reached = ((reached.astype(F32) + more) > 0.5).astype(BF16)
    diagonal_ones = (node_index[:, None] == node_index[None, :]).astype(F32)
    return jnp.minimum(diagonal_ones + reached.astype(F32) + reached.T.astype(F32), 1.0)


def body(hamiltonian, margin, pole_shift, row_map, parent):
    grid_rows = lax.axis_size("prow")
    grid_cols = lax.axis_size("pcol")
    my_row = lax.axis_index("prow")
    my_col = lax.axis_index("pcol")
    node_count = parent.shape[0]
    band = hamiltonian.shape[0]
    height = band * grid_cols
    width = hamiltonian.shape[1] // grid_cols
    row_slots, col_slots = height // SN, width // SN

    own = jnp.concatenate(
        [array[:, t * width : t * width + SN] for array in (hamiltonian, margin) for t in range(STEPS)],
        axis=1,
    )
    along_z = [[z * N_X + x for z in range(N_Z)] for x in range(N_X)]
    along_x = [[z * N_X + x for x in range(N_X)] for z in range(N_Z)]
    panel_z = lax.all_to_all(
        jnp.broadcast_to(own[None], (N_Z,) + own.shape), "pcol", 0, 0, axis_index_groups=along_z
    ).reshape(N_Z * band, -1)
    panel_raw = lax.all_to_all(
        jnp.broadcast_to(panel_z[None], (N_X,) + panel_z.shape),
        "pcol",
        0,
        0,
        axis_index_groups=along_x,
    ).reshape(height, -1)
    main = lax.all_to_all(
        jnp.concatenate(
            [array.reshape(band, grid_cols, width) for array in (hamiltonian, margin)], axis=0
        ),
        "pcol",
        split_axis=1,
        concat_axis=0,
        tiled=True,
    )
    pattern = structure(parent, node_count)
    row_nodes = jnp.arange(row_slots, dtype=jnp.int32) * grid_rows + my_row
    col_nodes = jnp.arange(col_slots, dtype=jnp.int32) * grid_cols + my_col
    all_nodes = jnp.arange(node_count, dtype=jnp.int32)
    pick_rows = (row_nodes[:, None] == all_nodes[None, :]).astype(F32)
    pick_cols = (col_nodes[:, None] == all_nodes[None, :]).astype(F32)
    row_pattern = jnp.dot(pick_rows, pattern)
    local_pattern = jnp.dot(row_pattern, pick_cols.T)
    panel_pattern = row_pattern[:, :STEPS]

    place = row_map - my_row * height
    source, inner = place // band, place % band
    panel_place = ((source % N_X) * N_Z + source // N_X) * band + inner
    smem = pl.BlockSpec(memory_space=pltpu.SMEM)
    vmem = pl.BlockSpec(memory_space=pltpu.VMEM)
    params = pltpu.CompilerParams(vmem_limit_bytes=40 * 1024 * 1024)
    which = jnp.stack([my_col, my_row, jnp.int32(grid_rows)]).astype(jnp.int32)

    panel = pl.pallas_call(
        permute_kernel,
        out_shape=jax.ShapeDtypeStruct(panel_raw.shape, BF16),
        in_specs=[vmem, smem, vmem],
        out_specs=vmem,
        compiler_params=params,
        name="permute_panel",
    )(panel_place[:, None], panel_pattern, panel_raw)

    both = ("prow", "pcol")

    def device(row, col):
        return row * grid_cols + col

    roots = [c % grid_rows for c in range(grid_cols)]
    pivot_rows = [
        lax.ppermute(
            panel[:SN], both, [(device(t, c), device(roots[c], c)) for c in range(grid_cols)]
        )
        for t in range(STEPS)
    ]
    slot = my_col // grid_rows
    row_blocks = [
        lax.dynamic_slice_in_dim(panel, (slot + half * (grid_cols // grid_rows)) * SN, SN, 0)
        for half in range(col_slots)
    ]
    w, u = pl.pallas_call(
        root_kernel,
        out_shape=(
            jax.ShapeDtypeStruct((2, STEPS * SN, width), BF16),
            jax.ShapeDtypeStruct((STEPS - 1, 2, SN, width), BF16),
        ),
        in_specs=[smem, smem] + [vmem] * 5,
        out_specs=(vmem, vmem),
        compiler_params=params,
        name="pivot_chain",
    )(pole_shift, which, *pivot_rows, *row_blocks)

    my_root = my_col % grid_rows
    offset = (my_row // 2 - my_root // 2) % (grid_rows // 2)
    same_core = my_row % 2 == my_root % 2
    early = [
        lax.ppermute(
            u[i - 1], both, [(device(roots[c], c), device(i, c)) for c in range(grid_cols)]
        )
        for i in range(1, STEPS)
    ]
    u_here = jnp.where(my_row == 1, early[0], early[1])
    u_here = jnp.where(my_row == 0, jnp.zeros_like(u_here), u_here)
    held = [0]
    chips = grid_rows // 2
    stride = chips // 2
    while stride:
        pairs = [
            (
                device((roots[c] + 2 * h) % grid_rows, c),
                device((roots[c] + 2 * (h + stride)) % grid_rows, c),
            )
            for c in range(grid_cols)
            for h in held
        ]
        came = lax.ppermute(w, both, pairs)
        new = [h + stride for h in held]
        takes = functools.reduce(jnp.logical_or, [offset == n for n in new]) & same_core
        w = jnp.where(takes, came, w)
        held = held + new
        stride //= 2
    pairs = [
        (
            device((roots[c] + 2 * h) % grid_rows, c),
            device(((roots[c] + 2 * h) % grid_rows) ^ 1, c),
        )
        for c in range(grid_cols)
        for h in held
    ]
    came = lax.ppermute(w, both, pairs)
    w = jnp.where(same_core, w, came)

    out = pl.pallas_call(
        final_kernel,
        out_shape=jax.ShapeDtypeStruct((2, height, width), F32),
        in_specs=[smem, smem, smem] + [vmem] * 5,
        out_specs=vmem,
        compiler_params=params,
        name="update",
    )(
        pole_shift,
        which,
        local_pattern,
        place[:, None],
        main.reshape(grid_cols, 2 * band, width),
        panel,
        w,
        u_here,
    )
    return out


def solution(mesh):
    return jax.shard_map(
        body,
        mesh=mesh,
        in_specs=(P(("prow", "pcol"), None), P(("prow", "pcol"), None), P("pole"), P("prow"), P()),
        out_specs=P("pole", "prow", "pcol"),
        check_vma=False,
    )
```

```python
import functools

import jax
import jax.numpy as jnp
from jax import lax
from jax.experimental import pallas as pl
from jax.experimental.pallas import tpu as pltpu
from jax.sharding import PartitionSpec as P

SN = 128
STEPS = 3
NSI = 4
NBW = 96
CB = 2
N_Z = 12
N_X = 4
F32 = jnp.float32
BF16 = jnp.bfloat16


def split(x):
    high = x.astype(BF16)
    return high, (x - high.astype(F32)).astype(BF16)


def embed(block):
    real, imag = block[:, :SN], block[:, SN:]
    return jnp.concatenate([block, jnp.concatenate([-imag, real], axis=1)], axis=0)


def times(left, right, passes=1):
    dot = functools.partial(jnp.dot, preferred_element_type=F32)
    if passes == 1:
        return dot(left.astype(BF16), embed(right.astype(BF16)))
    height = left.shape[0]
    left_high, left_low = split(left)
    right_high, right_low = split(right)
    both = dot(jnp.concatenate([left_high, left_low], axis=0), embed(right_high))
    return both[:height] + (both[height:] + dot(left_high, embed(right_low)))


def invert_pivot(pivot):
    row = lax.broadcasted_iota(jnp.int32, (SN, SN), 0)
    col = lax.broadcasted_iota(jnp.int32, (SN, SN), 1)
    eye = (row == col).astype(F32)
    real, imag = pivot[:, :SN], pivot[:, SN:]
    diag_real = jnp.sum(real * eye, axis=0, keepdims=True)
    diag_imag = jnp.sum(imag * eye, axis=0, keepdims=True)
    modulus = diag_real * diag_real + diag_imag * diag_imag
    inv_real, inv_imag = diag_real / modulus, -diag_imag / modulus
    res_real = eye - (real * inv_real - imag * inv_imag)
    res_imag = -(real * inv_imag + imag * inv_real)
    scale_real = jnp.sum(eye * inv_real, axis=1, keepdims=True)
    scale_imag = jnp.sum(eye * inv_imag, axis=1, keepdims=True)
    plus_real = eye + res_real
    approx = jnp.concatenate(
        [
            scale_real * plus_real - scale_imag * res_imag,
            scale_real * res_imag + scale_imag * plus_real,
        ],
        axis=1,
    )
    residue = jnp.concatenate([res_real, res_imag], axis=1)
    power = times(residue, residue, 3)
    for sweep in range(NSI - 2):
        both = times(jnp.concatenate([approx, power], axis=0), power, 3 if sweep == 0 else 1)
        approx, power = approx + both[:SN], both[SN:]
    return approx + times(approx, power)


def spread_kernel(ham_ref, over_ref, out_ref, own_ref, sems):
    stride = ham_ref.shape[1] // (NBW // CB)
    copies = []
    for k, ref in enumerate((ham_ref, over_ref)):
        for t in range(STEPS):
            piece = k * STEPS + t
            copies.append(
                pltpu.make_async_copy(
                    ref.at[:, t * stride : t * stride + SN],
                    own_ref.at[:, piece * SN : (piece + 1) * SN],
                    sems.at[piece],
                )
            )
    for copy in copies:
        copy.start()
    for copy in copies:
        copy.wait()
    for receiver in range(out_ref.shape[0]):
        out_ref[receiver] = own_ref[...]


def pick_rows(place, chunks):
    start, total = 0, None
    for chunk in chunks:
        length = chunk.shape[0]
        pick = (
            place - start == lax.broadcasted_iota(jnp.int32, (SN, length), 1)
        ).astype(BF16)
        part = jnp.dot(pick, chunk[...], preferred_element_type=F32)
        total = part if total is None else total + part
        start += length
    return total


def store_masked(out_ref, rows, got, mask_ref, slot):
    for part in range(2 * STEPS):
        cols = slice(part * SN, (part + 1) * SN)
        out_ref[rows, cols] = (got[:, cols] * mask_ref[slot, part % STEPS]).astype(BF16)


def early_kernel(slot_ref, mask_ref, place_ref, *refs):
    chunks, (own_ref, cross_ref) = refs[:-2], refs[-2:]
    place = place_ref[0:SN, :]
    store_masked(own_ref, slice(0, SN), pick_rows(place, chunks), mask_ref, 0)
    for half in range(cross_ref.shape[0] // SN):
        slot = slot_ref[half]
        place = place_ref[pl.ds(pl.multiple_of(slot * SN, SN), SN), :]
        rows = slice(half * SN, (half + 1) * SN)
        store_masked(cross_ref, rows, pick_rows(place, chunks), mask_ref, slot)


def panel_kernel(mask_ref, place_ref, *refs):
    chunks, out_ref = refs[:-1], refs[-1]
    for slot in range(out_ref.shape[0] // SN):
        rows = slice(slot * SN, (slot + 1) * SN)
        store_masked(out_ref, rows, pick_rows(place_ref[rows, :], chunks), mask_ref, slot)


def for_raw_rows(z_real, z_imag, blocks):
    real, imag = blocks
    return z_imag * imag - z_real * real, -z_real * imag - z_imag * real


def pivot_kernel(
    shift_ref,
    which_ref,
    a0_ref,
    a1_ref,
    a2_ref,
    solve_ref,
    early_ref,
    column_ref,
    factor_ref,
    rows_ref,
    sems,
):
    z_real, z_imag = shift_ref[0], shift_ref[1]
    my_col = which_ref[0]
    copies = [
        pltpu.make_async_copy(ref, rows_ref.at[t], sems.at[t])
        for t, ref in enumerate((a0_ref, a1_ref, a2_ref))
    ]
    for copy in copies:
        copy.start()
    for copy in copies:
        copy.wait()

    def block(t, step):
        ham = rows_ref[t, :, step * SN : (step + 1) * SN].astype(F32)
        over = rows_ref[t, :, (STEPS + step) * SN : (STEPS + step + 1) * SN].astype(F32)
        return jnp.concatenate([ham - z_real * over, -z_imag * over], axis=1)

    a = [[block(t, s) for s in range(STEPS)] for t in range(STEPS)]
    x, f, k = [], {}, {}
    for t in range(STEPS):
        x.append(invert_pivot(a[t][t]))
        if t == STEPS - 1:
            break
        below = times(jnp.concatenate([a[i][t] for i in range(t + 1, STEPS)], axis=0), x[t], 3)
        for s in range(t + 1, STEPS):
            f[s, t] = below[(s - t - 1) * SN : (s - t) * SN]
        for s in range(t + 1, STEPS):
            change = times(below, a[t][s], 3)
            for i in range(t + 1, STEPS):
                a[i][s] = a[i][s] - change[(i - t - 1) * SN : (i - t) * SN]
    k[0, 1] = -times(x[0], a[0][1])
    k[1, 2] = -times(x[1], a[1][2])
    k[0, 2] = times(k[0, 1], k[1, 2]) - times(x[0], a[0][2])
    g = {(t, t): x[t] for t in range(STEPS)}
    g[1, 0] = -times(x[1], f[1, 0])
    g[2, 1] = -times(x[2], f[2, 1])
    g[2, 0] = -times(g[2, 1], f[1, 0]) - times(x[2], f[2, 0])
    zero = jnp.zeros((SN, 2 * SN), F32)
    half = STEPS * SN

    def store(ref, t, parts, offset, stride):
        real = jnp.concatenate([p[:, :SN] for p in parts], axis=1)
        imag = jnp.concatenate([p[:, SN:] for p in parts], axis=1)
        rows = slice(t * SN, (t + 1) * SN)
        ref[rows, offset : offset + real.shape[1]] = real.astype(BF16)
        ref[rows, offset + stride : offset + stride + real.shape[1]] = imag.astype(BF16)
        rows = slice(half + t * SN, half + (t + 1) * SN)
        real, imag = for_raw_rows(z_real, z_imag, (real, imag))
        ref[rows, offset : offset + real.shape[1]] = real.astype(BF16)
        ref[rows, offset + stride : offset + stride + real.shape[1]] = imag.astype(BF16)

    for t in range(STEPS):
        parts = []
        for s in range(STEPS):
            total = g[t, s] if s <= t else None
            for i in range(max(t + 1, s), STEPS):
                term = times(k[t, i], g[i, s])
                total = term if total is None else total + term
            parts.append(total)
        store(solve_ref, t, parts, 0, half)
        for i in range(1, STEPS):
            store(early_ref, t, [-k[t, i] if i > t else zero], (i - 1) * 2 * SN, SN)
    for s in range(STEPS):
        total = zero
        for t in range(s, STEPS):
            total = jnp.where(my_col == t, g[t, s], total)
        column_ref[:, s * SN : (s + 1) * SN] = total[:, :SN].astype(BF16)
        column_ref[:, half + s * SN : half + (s + 1) * SN] = total[:, SN:].astype(BF16)
    factor_ref[0] = f[1, 0]
    factor_ref[1] = jnp.where(my_col == 0, f[2, 0], f[2, 1])


def solve_kernel(which_ref, cross_ref, solve_ref, column_ref, v_ref):
    v = jnp.dot(cross_ref[...], solve_ref[...], preferred_element_type=F32).astype(BF16)
    v_ref[SN:] = v[SN:]
    v_ref[:SN] = jnp.where(which_ref[0] < STEPS, column_ref[...], v[:SN])


def pivot_rows_kernel(which_ref, cross_ref, early_ref, factor_ref, u_ref):
    my_col = which_ref[0]
    change = jnp.dot(cross_ref[...], early_ref[...], preferred_element_type=F32)
    for i in range(STEPS - 1):
        for part in range(2):
            cols = slice((2 * i + part) * SN, (2 * i + part + 1) * SN)
            for half in range(cross_ref.shape[0] // SN):
                block = change[half * SN : (half + 1) * SN, cols].T
                if half == 0:
                    factor = factor_ref[i, :, part * SN : (part + 1) * SN]
                    block = jnp.where(my_col < i + 1, factor, block)
                u_ref[i, part, :, half * SN : (half + 1) * SN] = block.astype(BF16)


def is_factor(which_ref, slot, half):
    node = which_ref[1] + which_ref[2] * slot
    return (which_ref[0] < STEPS) & (node > which_ref[0]) if half == 0 else None


def assemble_kernel(shift_ref, which_ref, mask_ref, place_ref, main_ref, out_ref):
    z_real, z_imag = shift_ref[0], shift_ref[1]
    height, width = out_ref.shape[1], out_ref.shape[2]
    band = main_ref.shape[1] // 2
    ham_raw = main_ref[:, :band, :].reshape(height, width)
    over_raw = main_ref[:, band:, :].reshape(height, width)
    for slot in range(height // SN):
        rows = slice(slot * SN, (slot + 1) * SN)
        place = place_ref[rows, :]
        ham = pick_rows(place, [ham_raw])
        over = pick_rows(place, [over_raw])
        real, imag = ham - z_real * over, -z_imag * over
        for half in range(width // SN):
            cols = slice(half * SN, (half + 1) * SN)
            keep = mask_ref[slot, half]
            factor = is_factor(which_ref, slot, half)
            if factor is not None:
                keep = jnp.where(factor, 0.0, keep)
            out_ref[0, rows, cols] = real[:, cols] * keep
            out_ref[1, rows, cols] = imag[:, cols] * keep


def update_kernel(
    shift_ref, which_ref, base_ref, panel_ref, v_ref, v_other_ref, u1_ref, u2_ref, out_ref
):
    z_real, z_imag = shift_ref[0], shift_ref[1]
    my_row, own = which_ref[1], which_ref[3] > 0
    height, width = out_ref.shape[1], out_ref.shape[2]
    v = jnp.where(own, v_ref[...], v_other_ref[...])
    half_depth = v.shape[1] // 2
    v_real, v_imag = v[:, :half_depth], v[:, half_depth:]
    m_real, m_imag = for_raw_rows(z_real, z_imag, (v_real.astype(F32), v_imag.astype(F32)))
    v_all = jnp.concatenate(
        [
            jnp.concatenate([v_real, m_real.astype(BF16)], axis=1),
            jnp.concatenate([v_imag, m_imag.astype(BF16)], axis=1),
        ],
        axis=0,
    )
    for slot in range(height // SN):
        rows = slice(slot * SN, (slot + 1) * SN)
        change = lax.dot_general(
            panel_ref[rows, :], v_all, (((1,), (1,)), ((), ())), preferred_element_type=F32
        )
        for part in range(2):
            part_change = change[:, part * width : (part + 1) * width]
            if slot == 0:
                later = jnp.where(my_row == 1, u1_ref[part].astype(F32), part_change)
                later = jnp.where(my_row == 2, u2_ref[part].astype(F32), later)
                part_change = jnp.where(my_row == 0, 0.0, later)
            for half in range(width // SN):
                cols = slice(half * SN, (half + 1) * SN)
                factor = is_factor(which_ref, slot, half)
                sign = -1.0 if factor is None else jnp.where(factor, 1.0, -1.0)
                out_ref[part, rows, cols] = (
                    base_ref[part, rows, cols] + part_change[:, cols] * sign
                )


def structure(parent, node_count):
    node_index = jnp.arange(node_count, dtype=jnp.int32)
    reached = (parent[:, None] == node_index[None, :]).astype(BF16)
    for level_index in range(node_count.bit_length()):
        more = jnp.dot(reached, reached, preferred_element_type=F32)
        reached = ((reached.astype(F32) + more) > 0.5).astype(BF16)
    diagonal_ones = (node_index[:, None] == node_index[None, :]).astype(F32)
    return jnp.minimum(diagonal_ones + reached.astype(F32) + reached.T.astype(F32), 1.0)


def body(hamiltonian, margin, pole_shift, row_map, parent):
    grid_rows = lax.axis_size("prow")
    grid_cols = lax.axis_size("pcol")
    my_row = lax.axis_index("prow")
    my_col = lax.axis_index("pcol")
    node_count = parent.shape[0]
    band = hamiltonian.shape[0]
    height = band * grid_cols
    width = hamiltonian.shape[1] // grid_cols
    row_slots, col_slots = height // SN, width // SN

    smem = pl.BlockSpec(memory_space=pltpu.SMEM)
    vmem = pl.BlockSpec(memory_space=pltpu.VMEM)
    params = pltpu.CompilerParams(vmem_limit_bytes=20 * 1024 * 1024)
    both = ("prow", "pcol")

    def device(row, col):
        return row * grid_cols + col

    hbm = pl.BlockSpec(memory_space=pltpu.HBM)
    pieces = 2 * STEPS
    copies = pl.pallas_call(
        spread_kernel,
        out_shape=jax.ShapeDtypeStruct((N_Z, band, pieces * SN), BF16),
        in_specs=[hbm, hbm],
        out_specs=vmem,
        scratch_shapes=[
            pltpu.VMEM((band, pieces * SN), BF16),
            pltpu.SemaphoreType.DMA((pieces,)),
        ],
        compiler_params=params,
        name="spread",
    )(hamiltonian, margin)
    along_z = [[z * N_X + x for z in range(N_Z)] for x in range(N_X)]
    held_rows = N_Z * band
    mine = lax.all_to_all(copies, "pcol", 0, 0, axis_index_groups=along_z).reshape(held_rows, -1)

    hamiltonian, margin, mine = lax.optimization_barrier((hamiltonian, margin, mine))
    packed = jnp.concatenate(
        [array.reshape(band, grid_cols, width) for array in (hamiltonian, margin)], axis=0
    )

    def shift_x(array, by):
        return lax.ppermute(
            array, "pcol", [(c, c - c % N_X + (c % N_X + by) % N_X) for c in range(grid_cols)]
        )

    below, above = shift_x(mine, 1), shift_x(mine, -1)
    far_first = shift_x(below[: held_rows // 2], 1)
    far_last = shift_x(above[held_rows // 2 :], -1)
    chunks = [mine, above, far_first, far_last, below]
    main = lax.all_to_all(packed, "pcol", split_axis=1, concat_axis=0, tiled=True)
    pattern = structure(parent, node_count)
    row_nodes = jnp.arange(row_slots, dtype=jnp.int32) * grid_rows + my_row
    col_nodes = jnp.arange(col_slots, dtype=jnp.int32) * grid_cols + my_col
    all_nodes = jnp.arange(node_count, dtype=jnp.int32)
    pick_rows = (row_nodes[:, None] == all_nodes[None, :]).astype(F32)
    pick_cols = (col_nodes[:, None] == all_nodes[None, :]).astype(F32)
    row_pattern = jnp.dot(pick_rows, pattern)
    local_pattern = jnp.dot(row_pattern, pick_cols.T)
    panel_pattern = row_pattern[:, :STEPS]

    place = row_map - my_row * height
    source, inner = place // band, place % band
    distance = (source % N_X - my_col % N_X) % N_X
    panel_place = distance * held_rows + source // N_X * band + inner
    same_core = my_row % 2 == 0
    which = jnp.stack(
        [my_col, my_row, jnp.int32(grid_rows), same_core.astype(jnp.int32)]
    ).astype(jnp.int32)
    first_slot = my_col // grid_rows
    slots = jnp.stack([first_slot, first_slot + grid_cols // grid_rows]).astype(jnp.int32)

    depth = 2 * STEPS * SN
    own_rows, cross_rows = pl.pallas_call(
        early_kernel,
        out_shape=(
            jax.ShapeDtypeStruct((SN, depth), BF16),
            jax.ShapeDtypeStruct((width, depth), BF16),
        ),
        in_specs=[smem, smem, vmem] + [vmem] * len(chunks),
        out_specs=(vmem,) * 2,
        compiler_params=params,
        name="early_rows",
    )(slots, panel_pattern, panel_place[:, None], *chunks)
    panel = pl.pallas_call(
        panel_kernel,
        out_shape=jax.ShapeDtypeStruct((height, 2 * STEPS * SN), BF16),
        in_specs=[smem, vmem] + [vmem] * len(chunks),
        out_specs=vmem,
        compiler_params=params,
        name="panel_rows",
    )(panel_pattern, panel_place[:, None], *chunks)

    columns = range(grid_cols)
    pivot_rows = [own_rows] + [
        lax.ppermute(own_rows, both, [(device(t, c), device(0, c)) for c in columns])
        for t in range(1, STEPS)
    ]
    cross_rows = lax.ppermute(
        cross_rows, both, [(device(c % grid_rows, c), device(0, c)) for c in columns]
    )
    solve, early_solve, column, factor = pl.pallas_call(
        pivot_kernel,
        out_shape=(
            jax.ShapeDtypeStruct((depth, depth), BF16),
            jax.ShapeDtypeStruct((depth, 2 * (STEPS - 1) * SN), BF16),
            jax.ShapeDtypeStruct((SN, depth), BF16),
            jax.ShapeDtypeStruct((STEPS - 1, SN, 2 * SN), F32),
        ),
        in_specs=[smem, smem] + [pl.BlockSpec(memory_space=pl.ANY)] * STEPS,
        out_specs=(vmem,) * 4,
        scratch_shapes=[
            pltpu.VMEM((STEPS, SN, depth), BF16),
            pltpu.SemaphoreType.DMA((STEPS,)),
        ],
        compiler_params=params,
        name="pivots",
    )(pole_shift, which, *pivot_rows)
    w = pl.pallas_call(
        solve_kernel,
        out_shape=jax.ShapeDtypeStruct((width, depth), BF16),
        in_specs=[smem] + [vmem] * 3,
        out_specs=vmem,
        compiler_params=params,
        name="solve",
    )(which, cross_rows, solve, column)
    u = pl.pallas_call(
        pivot_rows_kernel,
        out_shape=jax.ShapeDtypeStruct((STEPS - 1, 2, SN, width), BF16),
        in_specs=[smem] + [vmem] * 3,
        out_specs=vmem,
        compiler_params=params,
        name="pivot_rows",
    )(which, cross_rows, early_solve, factor)

    offset = my_row // 2

    def along_y(array, hops):
        return lax.ppermute(
            array,
            both,
            [(device(2 * start, c), device(2 * end, c)) for c in columns for start, end in hops],
        )

    up, down = along_y(w, [(0, 3)]), along_y(w, [(0, 6)])
    w = jnp.where((offset == 3) & same_core, up, jnp.where((offset == 6) & same_core, down, w))
    up, down = along_y(w, [(0, 1), (3, 4)]), along_y(w, [(0, 7), (3, 2), (6, 5)])
    near = (offset == 1) | (offset == 4)
    kept = (offset == 0) | (offset == 3) | (offset == 6)
    w = jnp.where(kept, w, jnp.where(near, up, down))
    early = [
        lax.ppermute(u[i - 1], both, [(device(0, c), device(i, c)) for c in columns])
        for i in range(1, STEPS)
    ]
    base = pl.pallas_call(
        assemble_kernel,
        out_shape=jax.ShapeDtypeStruct((2, height, width), F32),
        in_specs=[smem, smem, smem] + [vmem] * 2,
        out_specs=vmem,
        compiler_params=params,
        name="assemble",
    )(pole_shift, which, local_pattern, place[:, None], main.reshape(grid_cols, 2 * band, width))
    w, base, panel, early = lax.optimization_barrier((w, base, panel, early))
    other = lax.ppermute(
        w,
        both,
        [(device(row, c), device(row + 1, c)) for c in columns for row in range(0, grid_rows, 2)],
    )
    return pl.pallas_call(
        update_kernel,
        out_shape=jax.ShapeDtypeStruct((2, height, width), F32),
        in_specs=[smem, smem] + [vmem] * 6,
        out_specs=vmem,
        compiler_params=params,
        name="update",
    )(pole_shift, which, base, panel, w, other, *early)


def solution(mesh):
    return jax.shard_map(
        body,
        mesh=mesh,
        in_specs=(P(("prow", "pcol"), None), P(("prow", "pcol"), None), P("pole"), P("prow"), P()),
        out_specs=P("pole", "prow", "pcol"),
        check_vma=False,
    )
```

```python
import functools

import jax
import jax.numpy as jnp
from jax import lax
from jax.experimental import pallas as pl
from jax.experimental.pallas import tpu as pltpu
from jax.sharding import PartitionSpec as P

SN = 128
STEPS = 3
NSI = 4
NBW = 96
CB = 2
N_Z = 12
N_X = 4
F32 = jnp.float32
BF16 = jnp.bfloat16


def split(x):
    high = x.astype(BF16)
    return high, (x - high.astype(F32)).astype(BF16)


def embed(block):
    real, imag = block[:, :SN], block[:, SN:]
    return jnp.concatenate([block, jnp.concatenate([-imag, real], axis=1)], axis=0)


def times(left, right, passes=1):
    dot = functools.partial(jnp.dot, preferred_element_type=F32)
    if passes == 1:
        return dot(left.astype(BF16), embed(right.astype(BF16)))
    height = left.shape[0]
    left_high, left_low = split(left)
    right_high, right_low = split(right)
    both = dot(jnp.concatenate([left_high, left_low], axis=0), embed(right_high))
    return both[:height] + (both[height:] + dot(left_high, embed(right_low)))


def invert_pivot(pivot):
    row = lax.broadcasted_iota(jnp.int32, (SN, SN), 0)
    col = lax.broadcasted_iota(jnp.int32, (SN, SN), 1)
    eye = (row == col).astype(F32)
    real, imag = pivot[:, :SN], pivot[:, SN:]
    diag_real = jnp.sum(real * eye, axis=0, keepdims=True)
    diag_imag = jnp.sum(imag * eye, axis=0, keepdims=True)
    modulus = diag_real * diag_real + diag_imag * diag_imag
    inv_real, inv_imag = diag_real / modulus, -diag_imag / modulus
    res_real = eye - (real * inv_real - imag * inv_imag)
    res_imag = -(real * inv_imag + imag * inv_real)
    scale_real = jnp.sum(eye * inv_real, axis=1, keepdims=True)
    scale_imag = jnp.sum(eye * inv_imag, axis=1, keepdims=True)
    plus_real = eye + res_real
    approx = jnp.concatenate(
        [
            scale_real * plus_real - scale_imag * res_imag,
            scale_real * res_imag + scale_imag * plus_real,
        ],
        axis=1,
    )
    residue = jnp.concatenate([res_real, res_imag], axis=1)
    power = times(residue, residue, 3)
    for sweep in range(NSI - 2):
        both = times(jnp.concatenate([approx, power], axis=0), power, 3 if sweep == 0 else 1)
        approx, power = approx + both[:SN], both[SN:]
    return approx + times(approx, power)


def spread_kernel(ham_ref, over_ref, out_ref, own_ref, sems):
    stride = ham_ref.shape[1] // (NBW // CB)
    copies = []
    for k, ref in enumerate((ham_ref, over_ref)):
        for t in range(STEPS):
            piece = k * STEPS + t
            copies.append(
                pltpu.make_async_copy(
                    ref.at[:, t * stride : t * stride + SN],
                    own_ref.at[:, piece * SN : (piece + 1) * SN],
                    sems.at[piece],
                )
            )
    for copy in copies:
        copy.start()
    for copy in copies:
        copy.wait()
    for receiver in range(out_ref.shape[0]):
        out_ref[receiver] = own_ref[...]


def pack_kernel(ham_ref, over_ref, out_ref):
    band, width = out_ref.shape[1] // 2, out_ref.shape[2]
    for col in range(out_ref.shape[0]):
        cols = slice(col * width, (col + 1) * width)
        out_ref[col, :band] = ham_ref[:, cols]
        out_ref[col, band:] = over_ref[:, cols]


def pick_rows(place, chunks):
    start, total = 0, None
    for chunk in chunks:
        length = chunk.shape[0]
        pick = (
            place - start == lax.broadcasted_iota(jnp.int32, (SN, length), 1)
        ).astype(BF16)
        part = jnp.dot(pick, chunk[...], preferred_element_type=F32)
        total = part if total is None else total + part
        start += length
    return total


def store_masked(out_ref, rows, got, mask_ref, slot):
    for part in range(2 * STEPS):
        cols = slice(part * SN, (part + 1) * SN)
        out_ref[rows, cols] = (got[:, cols] * mask_ref[slot, part % STEPS]).astype(BF16)


def early_kernel(slot_ref, mask_ref, place_ref, *refs):
    chunks, out_ref = refs[:-1], refs[-1]

    @pl.when(slot_ref[0] >= 0)
    def _():
        for block in range(out_ref.shape[0] // SN):
            slot = slot_ref[block]
            place = place_ref[pl.ds(pl.multiple_of(slot * SN, SN), SN), :]
            rows = slice(block * SN, (block + 1) * SN)
            store_masked(out_ref, rows, pick_rows(place, chunks), mask_ref, slot)


def panel_kernel(mask_ref, place_ref, *refs):
    chunks, out_ref = refs[:-1], refs[-1]
    for slot in range(out_ref.shape[0] // SN):
        rows = slice(slot * SN, (slot + 1) * SN)
        store_masked(out_ref, rows, pick_rows(place_ref[rows, :], chunks), mask_ref, slot)


def for_raw_rows(z_real, z_imag, blocks):
    real, imag = blocks
    return z_imag * imag - z_real * real, -z_real * imag - z_imag * real


def pivot_kernel(
    shift_ref, which_ref, a0_ref, a1_ref, a2_ref, solve_ref, special_ref, rows_ref, sems
):
    z_real, z_imag = shift_ref[0], shift_ref[1]
    my_col = which_ref[0]
    copies = [
        pltpu.make_async_copy(ref, rows_ref.at[t], sems.at[t])
        for t, ref in enumerate((a0_ref, a1_ref, a2_ref))
    ]
    for copy in copies:
        copy.start()
    for copy in copies:
        copy.wait()

    def block(t, step):
        ham = rows_ref[t, :, step * SN : (step + 1) * SN].astype(F32)
        over = rows_ref[t, :, (STEPS + step) * SN : (STEPS + step + 1) * SN].astype(F32)
        return jnp.concatenate([ham - z_real * over, -z_imag * over], axis=1)

    def stacked(lefts, right, passes=1):
        product = times(jnp.concatenate(lefts, axis=0), right, passes)
        return [product[i * SN : (i + 1) * SN] for i in range(len(lefts))]

    a = [[block(t, s) for s in range(STEPS)] for t in range(STEPS)]
    x0 = invert_pivot(a[0][0])
    f10, f20 = stacked([a[1][0], a[2][0]], x0, 3)
    change = stacked([f10, f20], a[0][1], 3)
    a11, a21 = a[1][1] - change[0], a[2][1] - change[1]
    change = stacked([f10, f20], a[0][2], 3)
    a12, a22 = a[1][2] - change[0], a[2][2] - change[1]
    x1 = invert_pivot(a11)
    f21 = times(a21, x1, 3)
    x2 = invert_pivot(a22 - times(f21, a12, 3))
    k01 = -times(x0, a[0][1])
    k12 = -times(x1, a12)
    k02 = times(k01, k12) - times(x0, a[0][2])
    h01 = times(k01, x1)
    h12, h02 = stacked([k12, k02], x2)
    by_f10 = stacked([f21, h01, x1], f10)
    back = by_f10[0] - f20
    by_back = stacked([h02, x2], back)
    by_f21 = stacked([h12, h02, x2], f21)
    m20 = by_back[1]
    solve = [
        [x0 - by_f10[1] + by_back[0], h01 - by_f21[1], h02],
        [times(k12, m20) - by_f10[2], x1 - by_f21[0], h12],
        [m20, -by_f21[2], x2],
    ]
    zero = jnp.zeros((SN, 2 * SN), F32)
    half = STEPS * SN

    def store(row, stride, parts):
        real = jnp.concatenate([p[:, :SN] for p in parts], axis=1)
        imag = jnp.concatenate([p[:, SN:] for p in parts], axis=1)
        over_real, over_imag = for_raw_rows(z_real, z_imag, (real, imag))
        for offset, ham, over in ((0, real, over_real), (stride, imag, over_imag)):
            rows = slice(row + offset, row + offset + SN)
            solve_ref[rows, :half] = ham.astype(BF16)
            solve_ref[rows, half:] = over.astype(BF16)

    for t in range(STEPS):
        store(t * SN, half, solve[t])
    store(2 * half, SN, [f10, zero, zero])
    store(2 * half + 2 * SN, SN, [-back, f21, zero])
    upper = [[x0, h01, h02], [zero, x1, h12], [zero, zero, x2]]
    for s in range(STEPS):
        total = jnp.where(my_col == 0, upper[s][0], upper[s][1])
        total = jnp.where(my_col == 2, upper[s][2], total)
        special_ref[s * SN : (s + 1) * SN, :] = total[:, :SN].astype(BF16)
        special_ref[half + s * SN : half + (s + 1) * SN, :] = total[:, SN:].astype(BF16)
    for i, total in enumerate((f10, jnp.where(my_col == 0, f20, f21))):
        row = 2 * half + 2 * i * SN
        special_ref[row : row + SN, :] = total[:, :SN].astype(BF16)
        special_ref[row + SN : row + 2 * SN, :] = total[:, SN:].astype(BF16)


def solve_kernel(which_ref, cross_ref, solve_ref, special_ref, w_ref, u1_ref, u2_ref):
    my_col = which_ref[0]
    start = 0
    for out_ref, limit in ((w_ref, STEPS), (u1_ref, 1), (u2_ref, 2)):
        rows = slice(start, start + out_ref.shape[0])
        got = lax.dot_general(
            solve_ref[rows, :],
            cross_ref[...],
            (((1,), (1,)), ((), ())),
            preferred_element_type=F32,
        ).astype(BF16)
        out_ref[:, SN:] = got[:, SN:]
        out_ref[:, :SN] = jnp.where(my_col < limit, special_ref[rows, :], got[:, :SN])
        start += out_ref.shape[0]


def is_factor(which_ref, slot, half):
    node = which_ref[1] + which_ref[2] * slot
    return (which_ref[0] < STEPS) & (node > which_ref[0]) if half == 0 else None


def assemble_kernel(shift_ref, which_ref, mask_ref, place_ref, main_ref, out_ref):
    z_real, z_imag = shift_ref[0], shift_ref[1]
    height, width = out_ref.shape[1], out_ref.shape[2]
    band = main_ref.shape[1] // 2
    ham_raw = main_ref[:, :band, :].reshape(height, width)
    over_raw = main_ref[:, band:, :].reshape(height, width)
    for slot in range(height // SN):
        rows = slice(slot * SN, (slot + 1) * SN)
        place = place_ref[rows, :]
        ham = pick_rows(place, [ham_raw])
        over = pick_rows(place, [over_raw])
        real, imag = ham - z_real * over, -z_imag * over
        for half in range(width // SN):
            cols = slice(half * SN, (half + 1) * SN)
            keep = mask_ref[slot, half]
            factor = is_factor(which_ref, slot, half)
            if factor is not None:
                keep = jnp.where(factor, 0.0, keep)
            out_ref[0, rows, cols] = real[:, cols] * keep
            out_ref[1, rows, cols] = imag[:, cols] * keep


def update_kernel(
    shift_ref,
    which_ref,
    base_ref,
    panel_ref,
    w_ref,
    w_other_ref,
    u1_ref,
    u2_ref,
    out_ref,
    done_ref,
    sems,
):
    z_real, z_imag = shift_ref[0], shift_ref[1]
    my_row, own = which_ref[1], which_ref[3] > 0
    height, width = out_ref.shape[1], out_ref.shape[2]
    w = jnp.where(own, w_ref[...], w_other_ref[...])
    half = w.shape[0] // 2
    over_real, over_imag = for_raw_rows(
        z_real, z_imag, (w[:half].astype(F32), w[half:].astype(F32))
    )
    w_all = jnp.concatenate(
        [
            jnp.concatenate([w[:half], w[half:]], axis=1),
            jnp.concatenate([over_real, over_imag], axis=1).astype(BF16),
        ],
        axis=0,
    )
    copies = []
    for slot in range(height // SN):
        rows = slice(slot * SN, (slot + 1) * SN)
        change = jnp.dot(panel_ref[rows, :], w_all, preferred_element_type=F32)
        for part in range(2):
            part_change = change[:, part * width : (part + 1) * width]
            if slot == 0:
                block = slice(part * SN, (part + 1) * SN)
                later = jnp.where(my_row == 1, u1_ref[block, :].astype(F32), part_change)
                later = jnp.where(my_row == 2, u2_ref[block, :].astype(F32), later)
                part_change = jnp.where(my_row == 0, 0.0, later)
            for piece in range(width // SN):
                cols = slice(piece * SN, (piece + 1) * SN)
                factor = is_factor(which_ref, slot, piece)
                sign = -1.0 if factor is None else jnp.where(factor, 1.0, -1.0)
                done_ref[part, rows, cols] = (
                    base_ref[part, rows, cols] + part_change[:, cols] * sign
                )
            copy = pltpu.make_async_copy(
                done_ref.at[part, rows], out_ref.at[part, rows], sems.at[slot, part]
            )
            copy.start()
            copies.append(copy)
    for copy in copies:
        copy.wait()


def structure(parent, node_count):
    node_index = jnp.arange(node_count, dtype=jnp.int32)
    reached = (parent[:, None] == node_index[None, :]).astype(BF16)
    for level_index in range(node_count.bit_length()):
        more = jnp.dot(reached, reached, preferred_element_type=F32)
        reached = ((reached.astype(F32) + more) > 0.5).astype(BF16)
    diagonal_ones = (node_index[:, None] == node_index[None, :]).astype(F32)
    return jnp.minimum(diagonal_ones + reached.astype(F32) + reached.T.astype(F32), 1.0)


def body(hamiltonian, margin, pole_shift, row_map, parent):
    grid_rows = lax.axis_size("prow")
    grid_cols = lax.axis_size("pcol")
    my_row = lax.axis_index("prow")
    my_col = lax.axis_index("pcol")
    node_count = parent.shape[0]
    band = hamiltonian.shape[0]
    height = band * grid_cols
    width = hamiltonian.shape[1] // grid_cols
    row_slots, col_slots = height // SN, width // SN

    smem = pl.BlockSpec(memory_space=pltpu.SMEM)
    vmem = pl.BlockSpec(memory_space=pltpu.VMEM)
    params = pltpu.CompilerParams(vmem_limit_bytes=20 * 1024 * 1024)
    full = pltpu.CompilerParams(vmem_limit_bytes=56 * 1024 * 1024)
    both = ("prow", "pcol")

    def device(row, col):
        return row * grid_cols + col

    hbm = pl.BlockSpec(memory_space=pltpu.HBM)
    pieces = 2 * STEPS
    copies = pl.pallas_call(
        spread_kernel,
        out_shape=jax.ShapeDtypeStruct((N_Z, band, pieces * SN), BF16),
        in_specs=[hbm, hbm],
        out_specs=vmem,
        scratch_shapes=[
            pltpu.VMEM((band, pieces * SN), BF16),
            pltpu.SemaphoreType.DMA((pieces,)),
        ],
        compiler_params=full,
        name="spread",
    )(hamiltonian, margin)
    along_z = [[z * N_X + x for z in range(N_Z)] for x in range(N_X)]
    held_rows = N_Z * band
    mine = lax.all_to_all(copies, "pcol", 0, 0, axis_index_groups=along_z).reshape(held_rows, -1)

    packed = pl.pallas_call(
        pack_kernel,
        out_shape=jax.ShapeDtypeStruct((grid_cols, 2 * band, width), BF16),
        in_specs=[vmem, vmem],
        out_specs=vmem,
        compiler_params=full,
        name="pack",
    )(hamiltonian, margin)
    packed, mine = lax.optimization_barrier((packed, mine))

    def shift_x(array, by):
        return lax.ppermute(
            array, "pcol", [(c, c - c % N_X + (c % N_X + by) % N_X) for c in range(grid_cols)]
        )

    below, above = shift_x(mine, 1), shift_x(mine, -1)
    far_first = shift_x(below[: held_rows // 2], 1)
    far_last = shift_x(above[held_rows // 2 :], -1)
    chunks = [mine, above, far_first, far_last, below]
    main = lax.all_to_all(packed, "pcol", 0, 0)
    pattern = structure(parent, node_count)
    row_nodes = jnp.arange(row_slots, dtype=jnp.int32) * grid_rows + my_row
    col_nodes = jnp.arange(col_slots, dtype=jnp.int32) * grid_cols + my_col
    all_nodes = jnp.arange(node_count, dtype=jnp.int32)
    pick_rows = (row_nodes[:, None] == all_nodes[None, :]).astype(F32)
    pick_cols = (col_nodes[:, None] == all_nodes[None, :]).astype(F32)
    row_pattern = jnp.dot(pick_rows, pattern)
    local_pattern = jnp.dot(row_pattern, pick_cols.T)
    panel_pattern = row_pattern[:, :STEPS]

    place = row_map - my_row * height
    source, inner = place // band, place % band
    distance = (source % N_X - my_col % N_X) % N_X
    panel_place = distance * held_rows + source // N_X * band + inner
    same_core = my_row % 2 == 0
    which = jnp.stack(
        [my_col, my_row, jnp.int32(grid_rows), same_core.astype(jnp.int32)]
    ).astype(jnp.int32)
    first_slot = my_col // grid_rows
    slots = jnp.stack([first_slot, first_slot + grid_cols // grid_rows]).astype(jnp.int32)

    depth = 2 * STEPS * SN

    def early_rows(slots, place, cost, name):
        return pl.pallas_call(
            early_kernel,
            out_shape=jax.ShapeDtypeStruct((slots.shape[0] * SN, depth), BF16),
            in_specs=[smem, smem, vmem] + [vmem] * len(chunks),
            out_specs=vmem,
            compiler_params=params,
            cost_estimate=pl.CostEstimate(
                flops=cost, bytes_accessed=4 * height * depth, transcendentals=0
            ),
            name=name,
        )(slots, panel_pattern, place, *chunks)

    panel_place = panel_place[:, None]
    columns = range(grid_cols)
    own_rows = early_rows(
        jnp.where(my_row < STEPS, 0, -1)[None].astype(jnp.int32), panel_place, 0, "own_rows"
    )
    pivot_rows = [
        lax.ppermute(own_rows, both, [(device(t, c), device(0, c)) for c in columns])
        for t in range(1, STEPS)
    ]
    panel = pl.pallas_call(
        panel_kernel,
        out_shape=jax.ShapeDtypeStruct((height, 2 * STEPS * SN), BF16),
        in_specs=[smem, vmem] + [vmem] * len(chunks),
        out_specs=vmem,
        compiler_params=params,
        name="panel_rows",
    )(panel_pattern, panel_place, *chunks)

    *pivot_rows, panel, later_place = lax.optimization_barrier((*pivot_rows, panel, panel_place))
    cross_rows = early_rows(
        jnp.where(my_row == my_col % grid_rows, slots, -1), later_place, 0, "cross_rows"
    )
    cross_rows = lax.ppermute(
        cross_rows, both, [(device(c % grid_rows, c), device(0, c)) for c in columns]
    )
    pivot_rows = [own_rows] + pivot_rows
    solve_height = depth + 2 * (STEPS - 1) * SN
    solve, special = pl.pallas_call(
        pivot_kernel,
        out_shape=(
            jax.ShapeDtypeStruct((solve_height, depth), BF16),
            jax.ShapeDtypeStruct((solve_height, SN), BF16),
        ),
        in_specs=[smem, smem] + [pl.BlockSpec(memory_space=pl.ANY)] * STEPS,
        out_specs=(vmem,) * 2,
        scratch_shapes=[
            pltpu.VMEM((STEPS, SN, depth), BF16),
            pltpu.SemaphoreType.DMA((STEPS,)),
        ],
        compiler_params=params,
        name="pivots",
    )(pole_shift, which, *pivot_rows)
    w, *u = pl.pallas_call(
        solve_kernel,
        out_shape=(
            jax.ShapeDtypeStruct((depth, width), BF16),
            jax.ShapeDtypeStruct((2 * SN, width), BF16),
            jax.ShapeDtypeStruct((2 * SN, width), BF16),
        ),
        in_specs=[smem] + [vmem] * 3,
        out_specs=(vmem,) * 3,
        compiler_params=params,
        name="solve",
    )(which, cross_rows, solve, special)

    offset = my_row // 2

    def along_y(array, hops):
        return lax.ppermute(
            array,
            both,
            [(device(2 * start, c), device(2 * end, c)) for c in columns for start, end in hops],
        )

    up, down = along_y(w, [(0, 3)]), along_y(w, [(0, 6)])
    w = jnp.where((offset == 3) & same_core, up, jnp.where((offset == 6) & same_core, down, w))
    up, down = along_y(w, [(0, 1), (3, 4)]), along_y(w, [(0, 7), (3, 2), (6, 5)])
    base = pl.pallas_call(
        assemble_kernel,
        out_shape=jax.ShapeDtypeStruct((2, height, width), F32),
        in_specs=[smem, smem, smem] + [vmem] * 2,
        out_specs=vmem,
        compiler_params=params,
        name="assemble",
    )(pole_shift, which, local_pattern, place[:, None], main)
    early = [
        lax.ppermute(u[i - 1], both, [(device(0, c), device(i, c)) for c in columns])
        for i in range(1, STEPS)
    ]
    up, down, early = lax.optimization_barrier((up, down, early))
    near = (offset == 1) | (offset == 4)
    kept = (offset == 0) | (offset == 3) | (offset == 6)
    w = jnp.where(kept, w, jnp.where(near, up, down))
    other = lax.ppermute(
        w,
        both,
        [(device(row, c), device(row + 1, c)) for c in columns for row in range(0, grid_rows, 2)],
    )
    return pl.pallas_call(
        update_kernel,
        out_shape=jax.ShapeDtypeStruct((2, height, width), F32),
        in_specs=[smem, smem] + [vmem] * 6,
        out_specs=pl.BlockSpec(memory_space=pl.ANY),
        scratch_shapes=[
            pltpu.VMEM((2, height, width), F32),
            pltpu.SemaphoreType.DMA((row_slots, 2)),
        ],
        compiler_params=params,
        name="update",
    )(pole_shift, which, base, panel, w, other, *early)


def solution(mesh):
    return jax.shard_map(
        body,
        mesh=mesh,
        in_specs=(P(("prow", "pcol"), None), P(("prow", "pcol"), None), P("pole"), P("prow"), P()),
        out_specs=P("pole", "prow", "pcol"),
        check_vma=False,
    )
```

```python
import functools

import jax
import jax.numpy as jnp
from jax import lax
from jax.experimental import pallas as pl
from jax.experimental.pallas import tpu as pltpu
from jax.sharding import PartitionSpec as P

SN = 128
STEPS = 3
NSI = 4
NBW = 96
CB = 2
N_Z = 12
N_X = 4
F32 = jnp.float32
BF16 = jnp.bfloat16


def split(x):
    high = x.astype(BF16)
    return high, (x - high.astype(F32)).astype(BF16)


def embed(block):
    real, imag = block[:, :SN], block[:, SN:]
    return jnp.concatenate([block, jnp.concatenate([-imag, real], axis=1)], axis=0)


def times(left, right, passes=1):
    dot = functools.partial(jnp.dot, preferred_element_type=F32)
    if passes == 1:
        return dot(left.astype(BF16), embed(right.astype(BF16)))
    height = left.shape[0]
    left_high, left_low = split(left)
    right_high, right_low = split(right)
    both = dot(jnp.concatenate([left_high, left_low], axis=0), embed(right_high))
    return both[:height] + (both[height:] + dot(left_high, embed(right_low)))


def invert_pivot(pivot):
    row = lax.broadcasted_iota(jnp.int32, (SN, SN), 0)
    col = lax.broadcasted_iota(jnp.int32, (SN, SN), 1)
    eye = (row == col).astype(F32)
    real, imag = pivot[:, :SN], pivot[:, SN:]
    diag_real = jnp.sum(real * eye, axis=0, keepdims=True)
    diag_imag = jnp.sum(imag * eye, axis=0, keepdims=True)
    modulus = diag_real * diag_real + diag_imag * diag_imag
    inv_real, inv_imag = diag_real / modulus, -diag_imag / modulus
    res_real = eye - (real * inv_real - imag * inv_imag)
    res_imag = -(real * inv_imag + imag * inv_real)
    scale_real = jnp.sum(eye * inv_real, axis=1, keepdims=True)
    scale_imag = jnp.sum(eye * inv_imag, axis=1, keepdims=True)
    plus_real = eye + res_real
    approx = jnp.concatenate(
        [
            scale_real * plus_real - scale_imag * res_imag,
            scale_real * res_imag + scale_imag * plus_real,
        ],
        axis=1,
    )
    residue = jnp.concatenate([res_real, res_imag], axis=1)
    power = times(residue, residue, 3)
    for sweep in range(NSI - 2):
        both = times(jnp.concatenate([approx, power], axis=0), power, 3 if sweep == 0 else 1)
        approx, power = approx + both[:SN], both[SN:]
    return approx + times(approx, power)


def spread_kernel(ham_ref, over_ref, out_ref, own_ref, sems):
    stride = ham_ref.shape[1] // (NBW // CB)
    copies = []
    for k, ref in enumerate((ham_ref, over_ref)):
        for t in range(STEPS):
            piece = k * STEPS + t
            copies.append(
                pltpu.make_async_copy(
                    ref.at[:, t * stride : t * stride + SN],
                    own_ref.at[:, piece * SN : (piece + 1) * SN],
                    sems.at[piece],
                )
            )
    for copy in copies:
        copy.start()
    for copy in copies:
        copy.wait()
    for receiver in range(out_ref.shape[0]):
        out_ref[receiver] = own_ref[...]


def pack_kernel(ham_ref, over_ref, out_ref):
    band, width = out_ref.shape[1] // 2, out_ref.shape[2]
    for col in range(out_ref.shape[0]):
        cols = slice(col * width, (col + 1) * width)
        out_ref[col, :band] = ham_ref[:, cols]
        out_ref[col, band:] = over_ref[:, cols]


def pick_rows(place, chunks):
    start, total = 0, None
    for chunk in chunks:
        length = chunk.shape[0]
        pick = (
            place - start == lax.broadcasted_iota(jnp.int32, (SN, length), 1)
        ).astype(BF16)
        part = jnp.dot(pick, chunk[...], preferred_element_type=F32)
        total = part if total is None else total + part
        start += length
    return total


def store_masked(out_ref, rows, got, mask_ref, slot):
    for part in range(2 * STEPS):
        cols = slice(part * SN, (part + 1) * SN)
        out_ref[rows, cols] = (got[:, cols] * mask_ref[slot, part % STEPS]).astype(BF16)


def early_kernel(slot_ref, mask_ref, place_ref, *refs):
    chunks, (own_ref, tail1_ref, tail2_ref, cross_ref) = refs[:-4], refs[-4:]

    @pl.when(slot_ref[0] >= 0)
    def _():
        got = pick_rows(place_ref[:SN, :], chunks)
        store_masked(own_ref, slice(0, SN), got, mask_ref, 0)
        for first, out_ref in ((1, tail1_ref), (2, tail2_ref)):
            length = (STEPS - first) * SN
            for part in range(2):
                start = (part * STEPS + first) * SN
                out_ref[:, part * length : (part + 1) * length] = own_ref[
                    :, start : start + length
                ]

    @pl.when(slot_ref[1] >= 0)
    def _():
        for block in range(cross_ref.shape[0] // SN):
            slot = slot_ref[1 + block]
            place = place_ref[pl.ds(pl.multiple_of(slot * SN, SN), SN), :]
            rows = slice(block * SN, (block + 1) * SN)
            store_masked(cross_ref, rows, pick_rows(place, chunks), mask_ref, slot)


def panel_kernel(mask_ref, place_ref, *refs):
    chunks, out_ref = refs[:-1], refs[-1]
    for slot in range(out_ref.shape[0] // SN):
        rows = slice(slot * SN, (slot + 1) * SN)
        store_masked(out_ref, rows, pick_rows(place_ref[rows, :], chunks), mask_ref, slot)


def for_raw_rows(z_real, z_imag, blocks):
    real, imag = blocks
    return z_imag * imag - z_real * real, -z_real * imag - z_imag * real


def shifted(shift_ref, ref, step, count):
    ham = ref[:, step * SN : (step + 1) * SN].astype(F32)
    over = ref[:, (count + step) * SN : (count + step + 1) * SN].astype(F32)
    return jnp.concatenate([ham - shift_ref[0] * over, -shift_ref[1] * over], axis=1)


def flip(block):
    return jnp.concatenate([block[:, :SN].T, block[:, SN:].T], axis=1)


def stacked(lefts, right, passes=1):
    product = times(jnp.concatenate(lefts, axis=0), right, passes)
    return [product[i * SN : (i + 1) * SN] for i in range(len(lefts))]


def first_pivot_kernel(shift_ref, own_ref, out_ref):
    a00, a01, a02 = [shifted(shift_ref, own_ref, s, STEPS) for s in range(STEPS)]
    x0 = invert_pivot(a00)
    f10, f20 = stacked([flip(a01), flip(a02)], x0, 3)
    out_ref[0], out_ref[1], out_ref[2] = x0, f10, f20
    out_ref[3] = times(f10, a01, 3)
    out_ref[4], out_ref[5] = stacked([f10, f20], a02, 3)


def pivot_kernel(shift_ref, which_ref, first_ref, a1_ref, a2_ref, solve_ref, special_ref):
    z_real, z_imag = shift_ref[0], shift_ref[1]
    my_col = which_ref[0]
    x0, f10, f20 = first_ref[0], first_ref[1], first_ref[2]
    a11 = shifted(shift_ref, a1_ref, 0, 2) - first_ref[3]
    a12 = shifted(shift_ref, a1_ref, 1, 2) - first_ref[4]
    a22 = shifted(shift_ref, a2_ref, 0, 1) - first_ref[5]
    x1 = invert_pivot(a11)
    f21 = times(flip(a12), x1, 3)
    x2 = invert_pivot(a22 - times(f21, a12, 3))
    k01, k12 = -flip(f10), -flip(f21)
    k02 = times(k01, k12) - flip(f20)
    h01 = times(k01, x1)
    h12, h02 = stacked([k12, k02], x2)
    by_f10 = stacked([f21, h01, x1], f10)
    back = by_f10[0] - f20
    by_back = stacked([h02, x2], back)
    by_f21 = stacked([h12, h02, x2], f21)
    m20 = by_back[1]
    solve = [
        [x0 - by_f10[1] + by_back[0], h01 - by_f21[1], h02],
        [times(k12, m20) - by_f10[2], x1 - by_f21[0], h12],
        [m20, -by_f21[2], x2],
    ]
    zero = jnp.zeros((SN, 2 * SN), F32)
    half = STEPS * SN

    def store(row, stride, parts):
        real = jnp.concatenate([p[:, :SN] for p in parts], axis=1)
        imag = jnp.concatenate([p[:, SN:] for p in parts], axis=1)
        over_real, over_imag = for_raw_rows(z_real, z_imag, (real, imag))
        for offset, ham, over in ((0, real, over_real), (stride, imag, over_imag)):
            rows = slice(row + offset, row + offset + SN)
            solve_ref[rows, :half] = ham.astype(BF16)
            solve_ref[rows, half:] = over.astype(BF16)

    for t in range(STEPS):
        store(t * SN, half, solve[t])
    store(2 * half, SN, [f10, zero, zero])
    store(2 * half + 2 * SN, SN, [-back, f21, zero])
    upper = [[x0, h01, h02], [zero, x1, h12], [zero, zero, x2]]
    for s in range(STEPS):
        total = jnp.where(my_col == 0, upper[s][0], upper[s][1])
        total = jnp.where(my_col == 2, upper[s][2], total)
        special_ref[s * SN : (s + 1) * SN, :] = total[:, :SN].astype(BF16)
        special_ref[half + s * SN : half + (s + 1) * SN, :] = total[:, SN:].astype(BF16)
    for i, total in enumerate((f10, jnp.where(my_col == 0, f20, f21))):
        row = 2 * half + 2 * i * SN
        special_ref[row : row + SN, :] = total[:, :SN].astype(BF16)
        special_ref[row + SN : row + 2 * SN, :] = total[:, SN:].astype(BF16)


def solve_kernel(which_ref, cross_ref, solve_ref, special_ref, w_ref, u1_ref, u2_ref):
    my_col = which_ref[0]
    start = 0
    for out_ref, limit in ((w_ref, STEPS), (u1_ref, 1), (u2_ref, 2)):
        rows = slice(start, start + out_ref.shape[0])
        got = lax.dot_general(
            solve_ref[rows, :],
            cross_ref[...],
            (((1,), (1,)), ((), ())),
            preferred_element_type=F32,
        ).astype(BF16)
        out_ref[:, SN:] = got[:, SN:]
        out_ref[:, :SN] = jnp.where(my_col < limit, special_ref[rows, :], got[:, :SN])
        start += out_ref.shape[0]


def is_factor(which_ref, slot, half):
    node = which_ref[1] + which_ref[2] * slot
    return (which_ref[0] < STEPS) & (node > which_ref[0]) if half == 0 else None


def assemble_kernel(shift_ref, which_ref, mask_ref, place_ref, main_ref, out_ref):
    z_real, z_imag = shift_ref[0], shift_ref[1]
    height, width = out_ref.shape[1], out_ref.shape[2]
    band = main_ref.shape[1] // 2
    ham_raw = main_ref[:, :band, :].reshape(height, width)
    over_raw = main_ref[:, band:, :].reshape(height, width)
    for slot in range(height // SN):
        rows = slice(slot * SN, (slot + 1) * SN)
        place = place_ref[rows, :]
        ham = pick_rows(place, [ham_raw])
        over = pick_rows(place, [over_raw])
        real, imag = ham - z_real * over, -z_imag * over
        for half in range(width // SN):
            cols = slice(half * SN, (half + 1) * SN)
            keep = mask_ref[slot, half]
            factor = is_factor(which_ref, slot, half)
            if factor is not None:
                keep = jnp.where(factor, 0.0, keep)
            out_ref[0, rows, cols] = real[:, cols] * keep
            out_ref[1, rows, cols] = imag[:, cols] * keep


def update_kernel(
    shift_ref,
    which_ref,
    base_ref,
    panel_ref,
    w_ref,
    w_other_ref,
    u1_ref,
    u2_ref,
    out_ref,
    done_ref,
    sems,
):
    z_real, z_imag = shift_ref[0], shift_ref[1]
    my_row, own = which_ref[1], which_ref[3] > 0
    height, width = out_ref.shape[1], out_ref.shape[2]
    w = jnp.where(own, w_ref[...], w_other_ref[...])
    half = w.shape[0] // 2
    over_real, over_imag = for_raw_rows(
        z_real, z_imag, (w[:half].astype(F32), w[half:].astype(F32))
    )
    w_all = jnp.concatenate(
        [
            jnp.concatenate([w[:half], w[half:]], axis=1),
            jnp.concatenate([over_real, over_imag], axis=1).astype(BF16),
        ],
        axis=0,
    )
    copies = []
    for slot in range(height // SN):
        rows = slice(slot * SN, (slot + 1) * SN)
        change = jnp.dot(panel_ref[rows, :], w_all, preferred_element_type=F32)
        for part in range(2):
            part_change = change[:, part * width : (part + 1) * width]
            if slot == 0:
                block = slice(part * SN, (part + 1) * SN)
                later = jnp.where(my_row == 1, u1_ref[block, :].astype(F32), part_change)
                later = jnp.where(my_row == 2, u2_ref[block, :].astype(F32), later)
                part_change = jnp.where(my_row == 0, 0.0, later)
            for piece in range(width // SN):
                cols = slice(piece * SN, (piece + 1) * SN)
                factor = is_factor(which_ref, slot, piece)
                sign = -1.0 if factor is None else jnp.where(factor, 1.0, -1.0)
                done_ref[part, rows, cols] = (
                    base_ref[part, rows, cols] + part_change[:, cols] * sign
                )
            copy = pltpu.make_async_copy(
                done_ref.at[part, rows], out_ref.at[part, rows], sems.at[slot, part]
            )
            copy.start()
            copies.append(copy)
    for copy in copies:
        copy.wait()


def structure(parent, node_count):
    node_index = jnp.arange(node_count, dtype=jnp.int32)
    reached = (parent[:, None] == node_index[None, :]).astype(BF16)
    for level_index in range(node_count.bit_length()):
        more = jnp.dot(reached, reached, preferred_element_type=F32)
        reached = ((reached.astype(F32) + more) > 0.5).astype(BF16)
    diagonal_ones = (node_index[:, None] == node_index[None, :]).astype(F32)
    return jnp.minimum(diagonal_ones + reached.astype(F32) + reached.T.astype(F32), 1.0)


def body(hamiltonian, margin, pole_shift, row_map, parent):
    grid_rows = lax.axis_size("prow")
    grid_cols = lax.axis_size("pcol")
    my_row = lax.axis_index("prow")
    my_col = lax.axis_index("pcol")
    node_count = parent.shape[0]
    band = hamiltonian.shape[0]
    height = band * grid_cols
    width = hamiltonian.shape[1] // grid_cols
    row_slots, col_slots = height // SN, width // SN

    smem = pl.BlockSpec(memory_space=pltpu.SMEM)
    vmem = pl.BlockSpec(memory_space=pltpu.VMEM)
    params = pltpu.CompilerParams(vmem_limit_bytes=20 * 1024 * 1024)
    full = pltpu.CompilerParams(vmem_limit_bytes=56 * 1024 * 1024)
    both = ("prow", "pcol")

    def device(row, col):
        return row * grid_cols + col

    hbm = pl.BlockSpec(memory_space=pltpu.HBM)
    pieces = 2 * STEPS
    copies = pl.pallas_call(
        spread_kernel,
        out_shape=jax.ShapeDtypeStruct((N_Z, band, pieces * SN), BF16),
        in_specs=[hbm, hbm],
        out_specs=vmem,
        scratch_shapes=[
            pltpu.VMEM((band, pieces * SN), BF16),
            pltpu.SemaphoreType.DMA((pieces,)),
        ],
        compiler_params=full,
        name="spread",
    )(hamiltonian, margin)
    along_z = [[z * N_X + x for z in range(N_Z)] for x in range(N_X)]
    held_rows = N_Z * band
    mine = lax.all_to_all(copies, "pcol", 0, 0, axis_index_groups=along_z).reshape(held_rows, -1)

    packed = pl.pallas_call(
        pack_kernel,
        out_shape=jax.ShapeDtypeStruct((grid_cols, 2 * band, width), BF16),
        in_specs=[vmem, vmem],
        out_specs=vmem,
        compiler_params=full,
        name="pack",
    )(hamiltonian, margin)
    packed, mine = lax.optimization_barrier((packed, mine))

    def shift_x(array, by):
        return lax.ppermute(
            array, "pcol", [(c, c - c % N_X + (c % N_X + by) % N_X) for c in range(grid_cols)]
        )

    below, above = shift_x(mine, 1), shift_x(mine, -1)
    far_first = shift_x(below[: held_rows // 2], 1)
    far_last = shift_x(above[held_rows // 2 :], -1)
    chunks = [mine, above, far_first, far_last, below]
    main = lax.all_to_all(packed, "pcol", 0, 0)
    pattern = structure(parent, node_count)
    row_nodes = jnp.arange(row_slots, dtype=jnp.int32) * grid_rows + my_row
    col_nodes = jnp.arange(col_slots, dtype=jnp.int32) * grid_cols + my_col
    all_nodes = jnp.arange(node_count, dtype=jnp.int32)
    pick_rows = (row_nodes[:, None] == all_nodes[None, :]).astype(F32)
    pick_cols = (col_nodes[:, None] == all_nodes[None, :]).astype(F32)
    row_pattern = jnp.dot(pick_rows, pattern)
    local_pattern = jnp.dot(row_pattern, pick_cols.T)
    panel_pattern = row_pattern[:, :STEPS]

    place = row_map - my_row * height
    source, inner = place // band, place % band
    distance = (source % N_X - my_col % N_X) % N_X
    panel_place = distance * held_rows + source // N_X * band + inner
    same_core = my_row % 2 == 0
    which = jnp.stack(
        [my_col, my_row, jnp.int32(grid_rows), same_core.astype(jnp.int32)]
    ).astype(jnp.int32)
    first_slot = my_col // grid_rows
    slots = jnp.stack([first_slot, first_slot + grid_cols // grid_rows]).astype(jnp.int32)

    depth = 2 * STEPS * SN
    panel_place = panel_place[:, None]
    columns = range(grid_cols)
    wanted = jnp.concatenate(
        [
            jnp.where(my_row < STEPS, 0, -1)[None].astype(jnp.int32),
            jnp.where(my_row == my_col % grid_rows, slots, -1),
        ]
    )
    own_rows, tail1, tail2, cross_rows = pl.pallas_call(
        early_kernel,
        out_shape=tuple(
            jax.ShapeDtypeStruct(shape, BF16)
            for shape in ((SN, depth), (SN, 4 * SN), (SN, 2 * SN), (width, depth))
        ),
        in_specs=[smem, smem, vmem] + [vmem] * len(chunks),
        out_specs=(vmem,) * 4,
        compiler_params=params,
        name="early_rows",
    )(wanted, panel_pattern, panel_place, *chunks)
    tails = [
        lax.ppermute(tail, both, [(device(t, c), device(0, c)) for c in columns])
        for t, tail in ((1, tail1), (2, tail2))
    ]
    cross_rows = lax.ppermute(
        cross_rows, both, [(device(c % grid_rows, c), device(0, c)) for c in columns]
    )
    first = pl.pallas_call(
        first_pivot_kernel,
        out_shape=jax.ShapeDtypeStruct((6, SN, 2 * SN), F32),
        in_specs=[smem, vmem],
        out_specs=vmem,
        compiler_params=params,
        name="first_pivot",
    )(pole_shift, own_rows)
    panel = pl.pallas_call(
        panel_kernel,
        out_shape=jax.ShapeDtypeStruct((height, 2 * STEPS * SN), BF16),
        in_specs=[smem, vmem] + [vmem] * len(chunks),
        out_specs=vmem,
        compiler_params=params,
        name="panel_rows",
    )(panel_pattern, panel_place, *chunks)

    *tails, panel, first = lax.optimization_barrier((*tails, panel, first))
    solve_height = depth + 2 * (STEPS - 1) * SN
    solve, special = pl.pallas_call(
        pivot_kernel,
        out_shape=(
            jax.ShapeDtypeStruct((solve_height, depth), BF16),
            jax.ShapeDtypeStruct((solve_height, SN), BF16),
        ),
        in_specs=[smem, smem] + [vmem] * 3,
        out_specs=(vmem,) * 2,
        compiler_params=params,
        name="pivots",
    )(pole_shift, which, first, *tails)
    w, *u = pl.pallas_call(
        solve_kernel,
        out_shape=(
            jax.ShapeDtypeStruct((depth, width), BF16),
            jax.ShapeDtypeStruct((2 * SN, width), BF16),
            jax.ShapeDtypeStruct((2 * SN, width), BF16),
        ),
        in_specs=[smem] + [vmem] * 3,
        out_specs=(vmem,) * 3,
        compiler_params=params,
        name="solve",
    )(which, cross_rows, solve, special)

    offset = my_row // 2

    def along_y(array, hops):
        return lax.ppermute(
            array,
            both,
            [(device(2 * start, c), device(2 * end, c)) for c in columns for start, end in hops],
        )

    up, down = along_y(w, [(0, 3)]), along_y(w, [(0, 6)])
    w = jnp.where((offset == 3) & same_core, up, jnp.where((offset == 6) & same_core, down, w))
    up, down = along_y(w, [(0, 1), (3, 4)]), along_y(w, [(0, 7), (3, 2), (6, 5)])
    base = pl.pallas_call(
        assemble_kernel,
        out_shape=jax.ShapeDtypeStruct((2, height, width), F32),
        in_specs=[smem, smem, smem] + [vmem] * 2,
        out_specs=vmem,
        compiler_params=params,
        name="assemble",
    )(pole_shift, which, local_pattern, place[:, None], main)
    early = [
        lax.ppermute(u[i - 1], both, [(device(0, c), device(i, c)) for c in columns])
        for i in range(1, STEPS)
    ]
    up, down, early = lax.optimization_barrier((up, down, early))
    near = (offset == 1) | (offset == 4)
    kept = (offset == 0) | (offset == 3) | (offset == 6)
    w = jnp.where(kept, w, jnp.where(near, up, down))
    other = lax.ppermute(
        w,
        both,
        [(device(row, c), device(row + 1, c)) for c in columns for row in range(0, grid_rows, 2)],
    )
    return pl.pallas_call(
        update_kernel,
        out_shape=jax.ShapeDtypeStruct((2, height, width), F32),
        in_specs=[smem, smem] + [vmem] * 6,
        out_specs=pl.BlockSpec(memory_space=pl.ANY),
        scratch_shapes=[
            pltpu.VMEM((2, height, width), F32),
            pltpu.SemaphoreType.DMA((row_slots, 2)),
        ],
        compiler_params=params,
        name="update",
    )(pole_shift, which, base, panel, w, other, *early)


def solution(mesh):
    return jax.shard_map(
        body,
        mesh=mesh,
        in_specs=(P(("prow", "pcol"), None), P(("prow", "pcol"), None), P("pole"), P("prow"), P()),
        out_specs=P("pole", "prow", "pcol"),
        check_vma=False,
    )
```

```python
import functools

import jax
import jax.numpy as jnp
from jax import lax
from jax.experimental import pallas as pl
from jax.experimental.pallas import tpu as pltpu
from jax.sharding import PartitionSpec as P

SN = 128
STEPS = 3
NSI = 4
NBW = 96
CB = 2
N_Z = 12
N_X = 4
F32 = jnp.float32
BF16 = jnp.bfloat16


def split(x):
    high = x.astype(BF16)
    return high, (x - high.astype(F32)).astype(BF16)


def embed(block):
    real, imag = block[:, :SN], block[:, SN:]
    return jnp.concatenate([block, jnp.concatenate([-imag, real], axis=1)], axis=0)


def times(left, right, passes=1):
    dot = functools.partial(jnp.dot, preferred_element_type=F32)
    if passes == 1:
        return dot(left.astype(BF16), embed(right.astype(BF16)))
    height = left.shape[0]
    left_high, left_low = split(left)
    right_high, right_low = split(right)
    both = dot(jnp.concatenate([left_high, left_low], axis=0), embed(right_high))
    return both[:height] + (both[height:] + dot(left_high, embed(right_low)))


def invert_pivot(pivot):
    row = lax.broadcasted_iota(jnp.int32, (SN, SN), 0)
    col = lax.broadcasted_iota(jnp.int32, (SN, SN), 1)
    eye = (row == col).astype(F32)
    real, imag = pivot[:, :SN], pivot[:, SN:]
    diag_real = jnp.sum(real * eye, axis=0, keepdims=True)
    diag_imag = jnp.sum(imag * eye, axis=0, keepdims=True)
    modulus = diag_real * diag_real + diag_imag * diag_imag
    inv_real, inv_imag = diag_real / modulus, -diag_imag / modulus
    res_real = eye - (real * inv_real - imag * inv_imag)
    res_imag = -(real * inv_imag + imag * inv_real)
    scale_real = jnp.sum(eye * inv_real, axis=1, keepdims=True)
    scale_imag = jnp.sum(eye * inv_imag, axis=1, keepdims=True)
    plus_real = eye + res_real
    approx = jnp.concatenate(
        [
            scale_real * plus_real - scale_imag * res_imag,
            scale_real * res_imag + scale_imag * plus_real,
        ],
        axis=1,
    )
    residue = jnp.concatenate([res_real, res_imag], axis=1)
    power = times(residue, residue, 3)
    for sweep in range(NSI - 2):
        both = times(jnp.concatenate([approx, power], axis=0), power, 3 if sweep == 0 else 1)
        approx, power = approx + both[:SN], both[SN:]
    return approx + times(approx, power)


def spread_kernel(ham_ref, over_ref, out_ref, own_ref, sems):
    stride = ham_ref.shape[1] // (NBW // CB)
    copies = []
    for k, ref in enumerate((ham_ref, over_ref)):
        for t in range(STEPS):
            piece = k * STEPS + t
            copies.append(
                pltpu.make_async_copy(
                    ref.at[:, t * stride : t * stride + SN],
                    own_ref.at[:, piece * SN : (piece + 1) * SN],
                    sems.at[piece],
                )
            )
    for copy in copies:
        copy.start()
    for copy in copies:
        copy.wait()
    for receiver in range(out_ref.shape[0]):
        out_ref[receiver] = own_ref[...]


def pack_kernel(ham_ref, over_ref, out_ref):
    band, width = out_ref.shape[1] // 2, out_ref.shape[2]
    for col in range(out_ref.shape[0]):
        cols = slice(col * width, (col + 1) * width)
        out_ref[col, :band] = ham_ref[:, cols]
        out_ref[col, band:] = over_ref[:, cols]


def pick_rows(place, chunks):
    start, total = 0, None
    for chunk in chunks:
        length = chunk.shape[0]
        pick = (
            place - start == lax.broadcasted_iota(jnp.int32, (SN, length), 1)
        ).astype(BF16)
        part = jnp.dot(pick, chunk[...], preferred_element_type=F32)
        total = part if total is None else total + part
        start += length
    return total


def store_masked(out_ref, rows, got, mask_ref, slot):
    for part in range(2 * STEPS):
        cols = slice(part * SN, (part + 1) * SN)
        out_ref[rows, cols] = (got[:, cols] * mask_ref[slot, part % STEPS]).astype(BF16)


def early_kernel(slot_ref, mask_ref, place_ref, *refs):
    chunks, (own_ref, tail1_ref, tail2_ref, cross_ref) = refs[:-4], refs[-4:]

    @pl.when(slot_ref[0] >= 0)
    def _():
        got = pick_rows(place_ref[:SN, :], chunks)
        store_masked(own_ref, slice(0, SN), got, mask_ref, 0)
        for first, out_ref in ((1, tail1_ref), (2, tail2_ref)):
            length = (STEPS - first) * SN
            for part in range(2):
                start = (part * STEPS + first) * SN
                out_ref[:, part * length : (part + 1) * length] = own_ref[
                    :, start : start + length
                ]

    @pl.when(slot_ref[1] >= 0)
    def _():
        for block in range(cross_ref.shape[0] // SN):
            slot = slot_ref[1 + block]
            place = place_ref[pl.ds(pl.multiple_of(slot * SN, SN), SN), :]
            rows = slice(block * SN, (block + 1) * SN)
            store_masked(cross_ref, rows, pick_rows(place, chunks), mask_ref, slot)


def panel_kernel(mask_ref, place_ref, *refs):
    chunks, out_ref = refs[:-1], refs[-1]
    for slot in range(out_ref.shape[0] // SN):
        rows = slice(slot * SN, (slot + 1) * SN)
        store_masked(out_ref, rows, pick_rows(place_ref[rows, :], chunks), mask_ref, slot)


def for_raw_rows(z_real, z_imag, blocks):
    real, imag = blocks
    return z_imag * imag - z_real * real, -z_real * imag - z_imag * real


def shifted(shift_ref, ref, step, count):
    ham = ref[:, step * SN : (step + 1) * SN].astype(F32)
    over = ref[:, (count + step) * SN : (count + step + 1) * SN].astype(F32)
    return jnp.concatenate([ham - shift_ref[0] * over, -shift_ref[1] * over], axis=1)


def flip(block):
    return jnp.concatenate([block[:, :SN].T, block[:, SN:].T], axis=1)


def stacked(lefts, right, passes=1):
    product = times(jnp.concatenate(lefts, axis=0), right, passes)
    return [product[i * SN : (i + 1) * SN] for i in range(len(lefts))]


def first_pivot_kernel(shift_ref, own_ref, out_ref):
    a00, a01, a02 = [shifted(shift_ref, own_ref, s, STEPS) for s in range(STEPS)]
    x0 = invert_pivot(a00)
    f10, f20 = stacked([flip(a01), flip(a02)], x0, 3)
    out_ref[0], out_ref[1], out_ref[2] = x0, f10, f20
    out_ref[3] = times(f10, a01, 3)
    out_ref[4], out_ref[5] = stacked([f10, f20], a02, 3)


def pivot_kernel(shift_ref, which_ref, first_ref, a1_ref, a2_ref, solve_ref, special_ref):
    z_real, z_imag = shift_ref[0], shift_ref[1]
    my_col = which_ref[0]
    x0, f10, f20 = first_ref[0], first_ref[1], first_ref[2]
    a11 = shifted(shift_ref, a1_ref, 0, 2) - first_ref[3]
    a12 = shifted(shift_ref, a1_ref, 1, 2) - first_ref[4]
    a22 = shifted(shift_ref, a2_ref, 0, 1) - first_ref[5]
    x1 = invert_pivot(a11)
    f21 = times(flip(a12), x1, 3)
    x2 = invert_pivot(a22 - times(f21, a12, 3))
    k01, k12 = -flip(f10), -flip(f21)
    k02 = times(k01, k12) - flip(f20)
    h01 = times(k01, x1)
    h12, h02 = stacked([k12, k02], x2)
    by_f10 = stacked([f21, h01, x1], f10)
    back = by_f10[0] - f20
    by_back = stacked([h02, x2], back)
    by_f21 = stacked([h12, h02, x2], f21)
    m20 = by_back[1]
    solve = [
        [x0 - by_f10[1] + by_back[0], h01 - by_f21[1], h02],
        [times(k12, m20) - by_f10[2], x1 - by_f21[0], h12],
        [m20, -by_f21[2], x2],
    ]
    zero = jnp.zeros((SN, 2 * SN), F32)
    half = STEPS * SN

    def store(row, stride, parts):
        real = jnp.concatenate([p[:, :SN] for p in parts], axis=1)
        imag = jnp.concatenate([p[:, SN:] for p in parts], axis=1)
        over_real, over_imag = for_raw_rows(z_real, z_imag, (real, imag))
        for offset, ham, over in ((0, real, over_real), (stride, imag, over_imag)):
            rows = slice(row + offset, row + offset + SN)
            solve_ref[rows, :half] = ham.astype(BF16)
            solve_ref[rows, half:] = over.astype(BF16)

    for t in range(STEPS):
        store(t * SN, half, solve[t])
    store(2 * half, SN, [f10, zero, zero])
    store(2 * half + 2 * SN, SN, [-back, f21, zero])
    upper = [[x0, h01, h02], [zero, x1, h12], [zero, zero, x2]]
    for s in range(STEPS):
        total = jnp.where(my_col == 0, upper[s][0], upper[s][1])
        total = jnp.where(my_col == 2, upper[s][2], total)
        special_ref[s * SN : (s + 1) * SN, :] = total[:, :SN].astype(BF16)
        special_ref[half + s * SN : half + (s + 1) * SN, :] = total[:, SN:].astype(BF16)
    for i, total in enumerate((f10, jnp.where(my_col == 0, f20, f21))):
        row = 2 * half + 2 * i * SN
        special_ref[row : row + SN, :] = total[:, :SN].astype(BF16)
        special_ref[row + SN : row + 2 * SN, :] = total[:, SN:].astype(BF16)


def solve_kernel(which_ref, cross_ref, solve_ref, special_ref, w_ref, u1_ref, u2_ref):
    my_col = which_ref[0]
    start = 0
    for out_ref, limit in ((w_ref, STEPS), (u1_ref, 1), (u2_ref, 2)):
        rows = slice(start, start + out_ref.shape[0])
        got = lax.dot_general(
            solve_ref[rows, :],
            cross_ref[...],
            (((1,), (1,)), ((), ())),
            preferred_element_type=F32,
        ).astype(BF16)
        out_ref[:, SN:] = got[:, SN:]
        out_ref[:, :SN] = jnp.where(my_col < limit, special_ref[rows, :], got[:, :SN])
        start += out_ref.shape[0]


def is_factor(which_ref, slot, half):
    node = which_ref[1] + which_ref[2] * slot
    return (which_ref[0] < STEPS) & (node > which_ref[0]) if half == 0 else None


def assemble_kernel(shift_ref, which_ref, mask_ref, place_ref, main_ref, out_ref):
    z_real, z_imag = shift_ref[0], shift_ref[1]
    height, width = out_ref.shape[1], out_ref.shape[2]
    band = main_ref.shape[1] // 2
    ham_raw = main_ref[:, :band, :].reshape(height, width)
    over_raw = main_ref[:, band:, :].reshape(height, width)
    for slot in range(height // SN):
        rows = slice(slot * SN, (slot + 1) * SN)
        place = place_ref[rows, :]
        ham = pick_rows(place, [ham_raw])
        over = pick_rows(place, [over_raw])
        real, imag = ham - z_real * over, -z_imag * over
        for half in range(width // SN):
            cols = slice(half * SN, (half + 1) * SN)
            keep = mask_ref[slot, half]
            factor = is_factor(which_ref, slot, half)
            if factor is not None:
                keep = jnp.where(factor, 0.0, keep)
            out_ref[0, rows, cols] = real[:, cols] * keep
            out_ref[1, rows, cols] = imag[:, cols] * keep


def update_kernel(
    shift_ref,
    which_ref,
    base_ref,
    panel_ref,
    w_ref,
    w_other_ref,
    u1_ref,
    u2_ref,
    out_ref,
    done_ref,
    sems,
):
    z_real, z_imag = shift_ref[0], shift_ref[1]
    my_row, own = which_ref[1], which_ref[3] > 0
    height, width = out_ref.shape[1], out_ref.shape[2]
    w = jnp.where(own, w_ref[...], w_other_ref[...])
    half = w.shape[0] // 2
    over_real, over_imag = for_raw_rows(
        z_real, z_imag, (w[:half].astype(F32), w[half:].astype(F32))
    )
    w_all = jnp.concatenate(
        [
            jnp.concatenate([w[:half], w[half:]], axis=1),
            jnp.concatenate([over_real, over_imag], axis=1).astype(BF16),
        ],
        axis=0,
    )
    copies = []
    for slot in range(height // SN):
        rows = slice(slot * SN, (slot + 1) * SN)
        change = jnp.dot(panel_ref[rows, :], w_all, preferred_element_type=F32)
        for part in range(2):
            part_change = change[:, part * width : (part + 1) * width]
            if slot == 0:
                block = slice(part * SN, (part + 1) * SN)
                later = jnp.where(my_row == 1, u1_ref[block, :].astype(F32), part_change)
                later = jnp.where(my_row == 2, u2_ref[block, :].astype(F32), later)
                part_change = jnp.where(my_row == 0, 0.0, later)
            for piece in range(width // SN):
                cols = slice(piece * SN, (piece + 1) * SN)
                factor = is_factor(which_ref, slot, piece)
                sign = -1.0 if factor is None else jnp.where(factor, 1.0, -1.0)
                done_ref[part, rows, cols] = (
                    base_ref[part, rows, cols] + part_change[:, cols] * sign
                )
            copy = pltpu.make_async_copy(
                done_ref.at[part, rows], out_ref.at[part, rows], sems.at[slot, part]
            )
            copy.start()
            copies.append(copy)
    for copy in copies:
        copy.wait()


def structure(parent, node_count):
    node_index = jnp.arange(node_count, dtype=jnp.int32)
    reached = (parent[:, None] == node_index[None, :]).astype(BF16)
    for level_index in range(node_count.bit_length()):
        more = jnp.dot(reached, reached, preferred_element_type=F32)
        reached = ((reached.astype(F32) + more) > 0.5).astype(BF16)
    diagonal_ones = (node_index[:, None] == node_index[None, :]).astype(F32)
    return jnp.minimum(diagonal_ones + reached.astype(F32) + reached.T.astype(F32), 1.0)


def body(hamiltonian, margin, pole_shift, row_map, parent):
    grid_rows = lax.axis_size("prow")
    grid_cols = lax.axis_size("pcol")
    my_row = lax.axis_index("prow")
    my_col = lax.axis_index("pcol")
    node_count = parent.shape[0]
    band = hamiltonian.shape[0]
    height = band * grid_cols
    width = hamiltonian.shape[1] // grid_cols
    row_slots, col_slots = height // SN, width // SN

    smem = pl.BlockSpec(memory_space=pltpu.SMEM)
    vmem = pl.BlockSpec(memory_space=pltpu.VMEM)
    params = pltpu.CompilerParams(vmem_limit_bytes=20 * 1024 * 1024)
    full = pltpu.CompilerParams(vmem_limit_bytes=56 * 1024 * 1024)
    both = ("prow", "pcol")

    def device(row, col):
        return row * grid_cols + col

    hbm = pl.BlockSpec(memory_space=pltpu.HBM)
    pieces = 2 * STEPS
    copies = pl.pallas_call(
        spread_kernel,
        out_shape=jax.ShapeDtypeStruct((N_Z, band, pieces * SN), BF16),
        in_specs=[hbm, hbm],
        out_specs=vmem,
        scratch_shapes=[
            pltpu.VMEM((band, pieces * SN), BF16),
            pltpu.SemaphoreType.DMA((pieces,)),
        ],
        compiler_params=full,
        name="spread",
    )(hamiltonian, margin)
    along_z = [[z * N_X + x for z in range(N_Z)] for x in range(N_X)]
    held_rows = N_Z * band
    mine = lax.all_to_all(copies, "pcol", 0, 0, axis_index_groups=along_z).reshape(held_rows, -1)

    packed = pl.pallas_call(
        pack_kernel,
        out_shape=jax.ShapeDtypeStruct((grid_cols, 2 * band, width), BF16),
        in_specs=[vmem, vmem],
        out_specs=vmem,
        compiler_params=full,
        name="pack",
    )(hamiltonian, margin)
    packed, mine = lax.optimization_barrier((packed, mine))

    def shift_x(array, by):
        return lax.ppermute(
            array, "pcol", [(c, c - c % N_X + (c % N_X + by) % N_X) for c in range(grid_cols)]
        )

    below, above = shift_x(mine, 1), shift_x(mine, -1)
    far_first = shift_x(below[: held_rows // 2], 1)
    far_last = shift_x(above[held_rows // 2 :], -1)
    chunks = [mine, above, far_first, far_last, below]
    main = lax.all_to_all(packed, "pcol", 0, 0)
    pattern = structure(parent, node_count)
    row_nodes = jnp.arange(row_slots, dtype=jnp.int32) * grid_rows + my_row
    col_nodes = jnp.arange(col_slots, dtype=jnp.int32) * grid_cols + my_col
    all_nodes = jnp.arange(node_count, dtype=jnp.int32)
    pick_rows = (row_nodes[:, None] == all_nodes[None, :]).astype(F32)
    pick_cols = (col_nodes[:, None] == all_nodes[None, :]).astype(F32)
    row_pattern = jnp.dot(pick_rows, pattern)
    local_pattern = jnp.dot(row_pattern, pick_cols.T)
    panel_pattern = row_pattern[:, :STEPS]

    place = row_map - my_row * height
    source, inner = place // band, place % band
    distance = (source % N_X - my_col % N_X) % N_X
    panel_place = distance * held_rows + source // N_X * band + inner
    same_core = my_row % 2 == 0
    which = jnp.stack(
        [my_col, my_row, jnp.int32(grid_rows), same_core.astype(jnp.int32)]
    ).astype(jnp.int32)
    first_slot = my_col // grid_rows
    slots = jnp.stack([first_slot, first_slot + grid_cols // grid_rows]).astype(jnp.int32)

    depth = 2 * STEPS * SN
    panel_place = panel_place[:, None]
    columns = range(grid_cols)
    wanted = jnp.concatenate(
        [
            jnp.where(my_row < STEPS, 0, -1)[None].astype(jnp.int32),
            jnp.where(my_row == my_col % grid_rows, slots, -1),
        ]
    )
    own_rows, tail1, tail2, cross_rows = pl.pallas_call(
        early_kernel,
        out_shape=tuple(
            jax.ShapeDtypeStruct(shape, BF16)
            for shape in ((SN, depth), (SN, 4 * SN), (SN, 2 * SN), (width, depth))
        ),
        in_specs=[smem, smem, vmem] + [vmem] * len(chunks),
        out_specs=(vmem,) * 4,
        compiler_params=params,
        name="early_rows",
    )(wanted, panel_pattern, panel_place, *chunks)
    tails = [
        lax.ppermute(tail, both, [(device(t, c), device(0, c)) for c in columns])
        for t, tail in ((1, tail1), (2, tail2))
    ]
    cross_rows = lax.ppermute(
        cross_rows, both, [(device(c % grid_rows, c), device(0, c)) for c in columns]
    )
    first = pl.pallas_call(
        first_pivot_kernel,
        out_shape=jax.ShapeDtypeStruct((6, SN, 2 * SN), F32),
        in_specs=[smem, vmem],
        out_specs=vmem,
        compiler_params=params,
        name="first_pivot",
    )(pole_shift, own_rows)
    panel = pl.pallas_call(
        panel_kernel,
        out_shape=jax.ShapeDtypeStruct((height, 2 * STEPS * SN), BF16),
        in_specs=[smem, vmem] + [vmem] * len(chunks),
        out_specs=vmem,
        compiler_params=params,
        name="panel_rows",
    )(panel_pattern, panel_place, *chunks)

    *tails, panel, first = lax.optimization_barrier((*tails, panel, first))
    solve_height = depth + 2 * (STEPS - 1) * SN
    solve, special = pl.pallas_call(
        pivot_kernel,
        out_shape=(
            jax.ShapeDtypeStruct((solve_height, depth), BF16),
            jax.ShapeDtypeStruct((solve_height, SN), BF16),
        ),
        in_specs=[smem, smem] + [vmem] * 3,
        out_specs=(vmem,) * 2,
        compiler_params=params,
        cost_estimate=pl.CostEstimate(flops=3000000000, bytes_accessed=10**6, transcendentals=0),
        name="pivots",
    )(pole_shift, which, first, *tails)
    w, *u = pl.pallas_call(
        solve_kernel,
        out_shape=(
            jax.ShapeDtypeStruct((depth, width), BF16),
            jax.ShapeDtypeStruct((2 * SN, width), BF16),
            jax.ShapeDtypeStruct((2 * SN, width), BF16),
        ),
        in_specs=[smem] + [vmem] * 3,
        out_specs=(vmem,) * 3,
        compiler_params=params,
        name="solve",
    )(which, cross_rows, solve, special)

    offset = my_row // 2

    def along_y(array, hops):
        return lax.ppermute(
            array,
            both,
            [(device(2 * start, c), device(2 * end, c)) for c in columns for start, end in hops],
        )

    up, down = along_y(w, [(0, 3)]), along_y(w, [(0, 6)])
    w = jnp.where((offset == 3) & same_core, up, jnp.where((offset == 6) & same_core, down, w))
    up, down = along_y(w, [(0, 1), (3, 4)]), along_y(w, [(0, 7), (3, 2), (6, 5)])
    base = pl.pallas_call(
        assemble_kernel,
        out_shape=jax.ShapeDtypeStruct((2, height, width), F32),
        in_specs=[smem, smem, smem] + [vmem] * 2,
        out_specs=vmem,
        compiler_params=params,
        name="assemble",
    )(pole_shift, which, local_pattern, place[:, None], main)
    early = [
        lax.ppermute(u[i - 1], both, [(device(0, c), device(i, c)) for c in columns])
        for i in range(1, STEPS)
    ]
    up, down, early = lax.optimization_barrier((up, down, early))
    near = (offset == 1) | (offset == 4)
    kept = (offset == 0) | (offset == 3) | (offset == 6)
    w = jnp.where(kept, w, jnp.where(near, up, down))
    other = lax.ppermute(
        w,
        both,
        [(device(row, c), device(row + 1, c)) for c in columns for row in range(0, grid_rows, 2)],
    )
    return pl.pallas_call(
        update_kernel,
        out_shape=jax.ShapeDtypeStruct((2, height, width), F32),
        in_specs=[smem, smem] + [vmem] * 6,
        out_specs=pl.BlockSpec(memory_space=pl.ANY),
        scratch_shapes=[
            pltpu.VMEM((2, height, width), F32),
            pltpu.SemaphoreType.DMA((row_slots, 2)),
        ],
        compiler_params=params,
        name="update",
    )(pole_shift, which, base, panel, w, other, *early)


def solution(mesh):
    return jax.shard_map(
        body,
        mesh=mesh,
        in_specs=(P(("prow", "pcol"), None), P(("prow", "pcol"), None), P("pole"), P("prow"), P()),
        out_specs=P("pole", "prow", "pcol"),
        check_vma=False,
    )
```

```python
import functools

import jax
import jax.numpy as jnp
from jax import lax
from jax.experimental import pallas as pl
from jax.experimental.pallas import tpu as pltpu
from jax.sharding import PartitionSpec as P

SN = 128
STEPS = 3
NSI = 4
NBW = 96
CB = 2
N_Z = 12
N_X = 4
F32 = jnp.float32
BF16 = jnp.bfloat16


def split(x):
    high = x.astype(BF16)
    return high, (x - high.astype(F32)).astype(BF16)


def embed(block):
    real, imag = block[:, :SN], block[:, SN:]
    return jnp.concatenate([block, jnp.concatenate([-imag, real], axis=1)], axis=0)


def times(left, right, passes=1):
    dot = functools.partial(jnp.dot, preferred_element_type=F32)
    if passes == 1:
        return dot(left.astype(BF16), embed(right.astype(BF16)))
    height = left.shape[0]
    left_high, left_low = split(left)
    right_high, right_low = split(right)
    both = dot(jnp.concatenate([left_high, left_low], axis=0), embed(right_high))
    return both[:height] + (both[height:] + dot(left_high, embed(right_low)))


def invert_pivot(pivot):
    row = lax.broadcasted_iota(jnp.int32, (SN, SN), 0)
    col = lax.broadcasted_iota(jnp.int32, (SN, SN), 1)
    eye = (row == col).astype(F32)
    real, imag = pivot[:, :SN], pivot[:, SN:]
    diag_real = jnp.sum(real * eye, axis=0, keepdims=True)
    diag_imag = jnp.sum(imag * eye, axis=0, keepdims=True)
    modulus = diag_real * diag_real + diag_imag * diag_imag
    inv_real, inv_imag = diag_real / modulus, -diag_imag / modulus
    res_real = eye - (real * inv_real - imag * inv_imag)
    res_imag = -(real * inv_imag + imag * inv_real)
    scale_real = jnp.sum(eye * inv_real, axis=1, keepdims=True)
    scale_imag = jnp.sum(eye * inv_imag, axis=1, keepdims=True)
    plus_real = eye + res_real
    approx = jnp.concatenate(
        [
            scale_real * plus_real - scale_imag * res_imag,
            scale_real * res_imag + scale_imag * plus_real,
        ],
        axis=1,
    )
    residue = jnp.concatenate([res_real, res_imag], axis=1)
    power = times(residue, residue, 3)
    for sweep in range(NSI - 2):
        both = times(jnp.concatenate([approx, power], axis=0), power, 3 if sweep == 0 else 1)
        approx, power = approx + both[:SN], both[SN:]
    return approx + times(approx, power)


def spread_kernel(ham_ref, over_ref, out_ref, own_ref, sems):
    stride = ham_ref.shape[1] // (NBW // CB)
    copies = []
    for k, ref in enumerate((ham_ref, over_ref)):
        for t in range(STEPS):
            piece = k * STEPS + t
            copies.append(
                pltpu.make_async_copy(
                    ref.at[:, t * stride : t * stride + SN],
                    own_ref.at[:, piece * SN : (piece + 1) * SN],
                    sems.at[piece],
                )
            )
    for copy in copies:
        copy.start()
    for copy in copies:
        copy.wait()
    for receiver in range(out_ref.shape[0]):
        out_ref[receiver] = own_ref[...]


def pack_kernel(ham_ref, over_ref, out_ref):
    band, width = out_ref.shape[1] // 2, out_ref.shape[2]
    for col in range(out_ref.shape[0]):
        cols = slice(col * width, (col + 1) * width)
        out_ref[col, :band] = ham_ref[:, cols]
        out_ref[col, band:] = over_ref[:, cols]


def pick_rows(place, chunks):
    start, total = 0, None
    for chunk in chunks:
        length = chunk.shape[0]
        pick = (
            place - start == lax.broadcasted_iota(jnp.int32, (SN, length), 1)
        ).astype(BF16)
        part = jnp.dot(pick, chunk[...], preferred_element_type=F32)
        total = part if total is None else total + part
        start += length
    return total


def store_masked(out_ref, rows, got, mask_ref, slot):
    for part in range(2 * STEPS):
        cols = slice(part * SN, (part + 1) * SN)
        out_ref[rows, cols] = (got[:, cols] * mask_ref[slot, part % STEPS]).astype(BF16)


def early_kernel(slot_ref, mask_ref, place_ref, *refs):
    chunks, (own_ref, tail1_ref, tail2_ref, cross_ref) = refs[:-4], refs[-4:]

    @pl.when(slot_ref[0] >= 0)
    def _():
        got = pick_rows(place_ref[:SN, :], chunks)
        store_masked(own_ref, slice(0, SN), got, mask_ref, 0)
        for first, out_ref in ((1, tail1_ref), (2, tail2_ref)):
            length = (STEPS - first) * SN
            for part in range(2):
                start = (part * STEPS + first) * SN
                out_ref[:, part * length : (part + 1) * length] = own_ref[
                    :, start : start + length
                ]

    @pl.when(slot_ref[1] >= 0)
    def _():
        for block in range(cross_ref.shape[0] // SN):
            slot = slot_ref[1 + block]
            place = place_ref[pl.ds(pl.multiple_of(slot * SN, SN), SN), :]
            rows = slice(block * SN, (block + 1) * SN)
            store_masked(cross_ref, rows, pick_rows(place, chunks), mask_ref, slot)


def panel_kernel(mask_ref, place_ref, *refs):
    chunks, out_ref = refs[:-1], refs[-1]
    for slot in range(out_ref.shape[0] // SN):
        rows = slice(slot * SN, (slot + 1) * SN)
        store_masked(out_ref, rows, pick_rows(place_ref[rows, :], chunks), mask_ref, slot)


def for_raw_rows(z_real, z_imag, blocks):
    real, imag = blocks
    return z_imag * imag - z_real * real, -z_real * imag - z_imag * real


def shifted(shift_ref, ref, step, count):
    ham = ref[:, step * SN : (step + 1) * SN].astype(F32)
    over = ref[:, (count + step) * SN : (count + step + 1) * SN].astype(F32)
    return jnp.concatenate([ham - shift_ref[0] * over, -shift_ref[1] * over], axis=1)


def flip(block):
    return jnp.concatenate([block[:, :SN].T, block[:, SN:].T], axis=1)


def stacked(lefts, right, passes=1):
    product = times(jnp.concatenate(lefts, axis=0), right, passes)
    return [product[i * SN : (i + 1) * SN] for i in range(len(lefts))]


def first_pivot_kernel(shift_ref, own_ref, out_ref):
    a00, a01, a02 = [shifted(shift_ref, own_ref, s, STEPS) for s in range(STEPS)]
    x0 = invert_pivot(a00)
    f10, f20 = stacked([flip(a01), flip(a02)], x0, 3)
    out_ref[0], out_ref[1], out_ref[2] = x0, f10, f20
    out_ref[3] = times(f10, a01, 3)
    out_ref[4], out_ref[5] = stacked([f10, f20], a02, 3)


def pivot_kernel(shift_ref, which_ref, first_ref, a1_ref, a2_ref, solve_ref, special_ref):
    z_real, z_imag = shift_ref[0], shift_ref[1]
    my_col = which_ref[0]
    x0, f10, f20 = first_ref[0], first_ref[1], first_ref[2]
    a11 = shifted(shift_ref, a1_ref, 0, 2) - first_ref[3]
    a12 = shifted(shift_ref, a1_ref, 1, 2) - first_ref[4]
    a22 = shifted(shift_ref, a2_ref, 0, 1) - first_ref[5]
    x1 = invert_pivot(a11)
    f21 = times(flip(a12), x1, 3)
    x2 = invert_pivot(a22 - times(f21, a12, 3))
    k01, k12 = -flip(f10), -flip(f21)
    k02 = times(k01, k12) - flip(f20)
    h01 = times(k01, x1)
    h12, h02 = stacked([k12, k02], x2)
    by_f10 = stacked([f21, h01, x1], f10)
    back = by_f10[0] - f20
    by_back = stacked([h02, x2], back)
    by_f21 = stacked([h12, h02, x2], f21)
    m20 = by_back[1]
    solve = [
        [x0 - by_f10[1] + by_back[0], h01 - by_f21[1], h02],
        [times(k12, m20) - by_f10[2], x1 - by_f21[0], h12],
        [m20, -by_f21[2], x2],
    ]
    zero = jnp.zeros((SN, 2 * SN), F32)
    half = STEPS * SN

    def store(row, stride, parts):
        real = jnp.concatenate([p[:, :SN] for p in parts], axis=1)
        imag = jnp.concatenate([p[:, SN:] for p in parts], axis=1)
        over_real, over_imag = for_raw_rows(z_real, z_imag, (real, imag))
        for offset, ham, over in ((0, real, over_real), (stride, imag, over_imag)):
            rows = slice(row + offset, row + offset + SN)
            solve_ref[rows, :half] = ham.astype(BF16)
            solve_ref[rows, half:] = over.astype(BF16)

    for t in range(STEPS):
        store(t * SN, half, solve[t])
    store(2 * half, SN, [f10, zero, zero])
    store(2 * half + 2 * SN, SN, [-back, f21, zero])
    upper = [[x0, h01, h02], [zero, x1, h12], [zero, zero, x2]]
    for s in range(STEPS):
        total = jnp.where(my_col == 0, upper[s][0], upper[s][1])
        total = jnp.where(my_col == 2, upper[s][2], total)
        special_ref[s * SN : (s + 1) * SN, :] = total[:, :SN].astype(BF16)
        special_ref[half + s * SN : half + (s + 1) * SN, :] = total[:, SN:].astype(BF16)
    for i, total in enumerate((f10, jnp.where(my_col == 0, f20, f21))):
        row = 2 * half + 2 * i * SN
        special_ref[row : row + SN, :] = total[:, :SN].astype(BF16)
        special_ref[row + SN : row + 2 * SN, :] = total[:, SN:].astype(BF16)


def solve_kernel(which_ref, cross_ref, solve_ref, special_ref, w_ref, u1_ref, u2_ref):
    my_col = which_ref[0]
    start = 0
    for out_ref, limit in ((w_ref, STEPS), (u1_ref, 1), (u2_ref, 2)):
        rows = slice(start, start + out_ref.shape[0])
        got = lax.dot_general(
            solve_ref[rows, :],
            cross_ref[...],
            (((1,), (1,)), ((), ())),
            preferred_element_type=F32,
        ).astype(BF16)
        out_ref[:, SN:] = got[:, SN:]
        out_ref[:, :SN] = jnp.where(my_col < limit, special_ref[rows, :], got[:, :SN])
        start += out_ref.shape[0]


def is_factor(which_ref, slot, half):
    node = which_ref[1] + which_ref[2] * slot
    return (which_ref[0] < STEPS) & (node > which_ref[0]) if half == 0 else None


def assemble_kernel(shift_ref, which_ref, mask_ref, place_ref, main_ref, out_ref):
    z_real, z_imag = shift_ref[0], shift_ref[1]
    height, width = out_ref.shape[1], out_ref.shape[2]
    band = main_ref.shape[1] // 2
    ham_raw = main_ref[:, :band, :].reshape(height, width)
    over_raw = main_ref[:, band:, :].reshape(height, width)
    for slot in range(height // SN):
        rows = slice(slot * SN, (slot + 1) * SN)
        place = place_ref[rows, :]
        ham = pick_rows(place, [ham_raw])
        over = pick_rows(place, [over_raw])
        real, imag = ham - z_real * over, -z_imag * over
        for half in range(width // SN):
            cols = slice(half * SN, (half + 1) * SN)
            keep = mask_ref[slot, half]
            factor = is_factor(which_ref, slot, half)
            if factor is not None:
                keep = jnp.where(factor, 0.0, keep)
            out_ref[0, rows, cols] = real[:, cols] * keep
            out_ref[1, rows, cols] = imag[:, cols] * keep


def pick_kernel(which_ref, first_ref, second_ref, third_ref, out_ref, sem):
    for index, ref in enumerate((first_ref, second_ref, third_ref)):

        @pl.when(which_ref[0] == index)
        def _():
            copy = pltpu.make_async_copy(ref, out_ref, sem)
            copy.start()
            copy.wait()


def update_kernel(
    shift_ref,
    which_ref,
    base_ref,
    panel_ref,
    w_ref,
    w_other_ref,
    u1_ref,
    u2_ref,
    out_ref,
    done_ref,
    sems,
):
    z_real, z_imag = shift_ref[0], shift_ref[1]
    my_row, own = which_ref[1], which_ref[3] > 0
    height, width = out_ref.shape[1], out_ref.shape[2]
    w = jnp.where(own, w_ref[...], w_other_ref[...])
    half = w.shape[0] // 2
    over_real, over_imag = for_raw_rows(
        z_real, z_imag, (w[:half].astype(F32), w[half:].astype(F32))
    )
    w_all = jnp.concatenate(
        [
            jnp.concatenate([w[:half], w[half:]], axis=1),
            jnp.concatenate([over_real, over_imag], axis=1).astype(BF16),
        ],
        axis=0,
    )
    copies = []
    for slot in range(height // SN):
        rows = slice(slot * SN, (slot + 1) * SN)
        change = jnp.dot(panel_ref[rows, :], w_all, preferred_element_type=F32)
        for part in range(2):
            part_change = change[:, part * width : (part + 1) * width]
            if slot == 0:
                block = slice(part * SN, (part + 1) * SN)
                later = jnp.where(my_row == 1, u1_ref[block, :].astype(F32), part_change)
                later = jnp.where(my_row == 2, u2_ref[block, :].astype(F32), later)
                part_change = jnp.where(my_row == 0, 0.0, later)
            for piece in range(width // SN):
                cols = slice(piece * SN, (piece + 1) * SN)
                factor = is_factor(which_ref, slot, piece)
                sign = -1.0 if factor is None else jnp.where(factor, 1.0, -1.0)
                done_ref[part, rows, cols] = (
                    base_ref[part, rows, cols] + part_change[:, cols] * sign
                )
            copy = pltpu.make_async_copy(
                done_ref.at[part, rows], out_ref.at[part, rows], sems.at[slot, part]
            )
            copy.start()
            copies.append(copy)
    for copy in copies:
        copy.wait()


def structure(parent, node_count):
    node_index = jnp.arange(node_count, dtype=jnp.int32)
    reached = (parent[:, None] == node_index[None, :]).astype(BF16)
    for level_index in range(node_count.bit_length()):
        more = jnp.dot(reached, reached, preferred_element_type=F32)
        reached = ((reached.astype(F32) + more) > 0.5).astype(BF16)
    diagonal_ones = (node_index[:, None] == node_index[None, :]).astype(F32)
    return jnp.minimum(diagonal_ones + reached.astype(F32) + reached.T.astype(F32), 1.0)


def body(hamiltonian, margin, pole_shift, row_map, parent):
    grid_rows = lax.axis_size("prow")
    grid_cols = lax.axis_size("pcol")
    my_row = lax.axis_index("prow")
    my_col = lax.axis_index("pcol")
    node_count = parent.shape[0]
    band = hamiltonian.shape[0]
    height = band * grid_cols
    width = hamiltonian.shape[1] // grid_cols
    row_slots, col_slots = height // SN, width // SN

    smem = pl.BlockSpec(memory_space=pltpu.SMEM)
    vmem = pl.BlockSpec(memory_space=pltpu.VMEM)
    params = pltpu.CompilerParams(vmem_limit_bytes=20 * 1024 * 1024)
    full = pltpu.CompilerParams(vmem_limit_bytes=56 * 1024 * 1024)
    both = ("prow", "pcol")

    def device(row, col):
        return row * grid_cols + col

    hbm = pl.BlockSpec(memory_space=pltpu.HBM)
    pieces = 2 * STEPS
    copies = pl.pallas_call(
        spread_kernel,
        out_shape=jax.ShapeDtypeStruct((N_Z, band, pieces * SN), BF16),
        in_specs=[hbm, hbm],
        out_specs=vmem,
        scratch_shapes=[
            pltpu.VMEM((band, pieces * SN), BF16),
            pltpu.SemaphoreType.DMA((pieces,)),
        ],
        compiler_params=full,
        name="spread",
    )(hamiltonian, margin)
    along_z = [[z * N_X + x for z in range(N_Z)] for x in range(N_X)]
    held_rows = N_Z * band
    mine = lax.all_to_all(copies, "pcol", 0, 0, axis_index_groups=along_z).reshape(held_rows, -1)

    packed = pl.pallas_call(
        pack_kernel,
        out_shape=jax.ShapeDtypeStruct((grid_cols, 2 * band, width), BF16),
        in_specs=[vmem, vmem],
        out_specs=vmem,
        compiler_params=full,
        name="pack",
    )(hamiltonian, margin)
    packed, mine = lax.optimization_barrier((packed, mine))

    def shift_x(array, by):
        return lax.ppermute(
            array, "pcol", [(c, c - c % N_X + (c % N_X + by) % N_X) for c in range(grid_cols)]
        )

    below, above = shift_x(mine, 1), shift_x(mine, -1)
    far_first = shift_x(below[: held_rows // 2], 1)
    far_last = shift_x(above[held_rows // 2 :], -1)
    chunks = [mine, above, far_first, far_last, below]
    main = lax.all_to_all(packed, "pcol", 0, 0)
    pattern = structure(parent, node_count)
    row_nodes = jnp.arange(row_slots, dtype=jnp.int32) * grid_rows + my_row
    col_nodes = jnp.arange(col_slots, dtype=jnp.int32) * grid_cols + my_col
    all_nodes = jnp.arange(node_count, dtype=jnp.int32)
    pick_rows = (row_nodes[:, None] == all_nodes[None, :]).astype(F32)
    pick_cols = (col_nodes[:, None] == all_nodes[None, :]).astype(F32)
    row_pattern = jnp.dot(pick_rows, pattern)
    local_pattern = jnp.dot(row_pattern, pick_cols.T)
    panel_pattern = row_pattern[:, :STEPS]

    place = row_map - my_row * height
    source, inner = place // band, place % band
    distance = (source % N_X - my_col % N_X) % N_X
    panel_place = distance * held_rows + source // N_X * band + inner
    same_core = my_row % 2 == 0
    which = jnp.stack(
        [my_col, my_row, jnp.int32(grid_rows), same_core.astype(jnp.int32)]
    ).astype(jnp.int32)
    first_slot = my_col // grid_rows
    slots = jnp.stack([first_slot, first_slot + grid_cols // grid_rows]).astype(jnp.int32)

    depth = 2 * STEPS * SN
    panel_place = panel_place[:, None]
    columns = range(grid_cols)
    wanted = jnp.concatenate(
        [
            jnp.where(my_row < STEPS, 0, -1)[None].astype(jnp.int32),
            jnp.where(my_row == my_col % grid_rows, slots, -1),
        ]
    )
    own_rows, tail1, tail2, cross_rows = pl.pallas_call(
        early_kernel,
        out_shape=tuple(
            jax.ShapeDtypeStruct(shape, BF16)
            for shape in ((SN, depth), (SN, 4 * SN), (SN, 2 * SN), (width, depth))
        ),
        in_specs=[smem, smem, vmem] + [vmem] * len(chunks),
        out_specs=(vmem,) * 4,
        compiler_params=params,
        name="early_rows",
    )(wanted, panel_pattern, panel_place, *chunks)
    tails = [
        lax.ppermute(tail, both, [(device(t, c), device(0, c)) for c in columns])
        for t, tail in ((1, tail1), (2, tail2))
    ]
    cross_rows = lax.ppermute(
        cross_rows, both, [(device(c % grid_rows, c), device(0, c)) for c in columns]
    )
    first = pl.pallas_call(
        first_pivot_kernel,
        out_shape=jax.ShapeDtypeStruct((6, SN, 2 * SN), F32),
        in_specs=[smem, vmem],
        out_specs=vmem,
        compiler_params=params,
        name="first_pivot",
    )(pole_shift, own_rows)
    panel = pl.pallas_call(
        panel_kernel,
        out_shape=jax.ShapeDtypeStruct((height, 2 * STEPS * SN), BF16),
        in_specs=[smem, vmem] + [vmem] * len(chunks),
        out_specs=vmem,
        compiler_params=params,
        name="panel_rows",
    )(panel_pattern, panel_place, *chunks)

    *tails, panel, first = lax.optimization_barrier((*tails, panel, first))
    solve_height = depth + 2 * (STEPS - 1) * SN
    solve, special = pl.pallas_call(
        pivot_kernel,
        out_shape=(
            jax.ShapeDtypeStruct((solve_height, depth), BF16),
            jax.ShapeDtypeStruct((solve_height, SN), BF16),
        ),
        in_specs=[smem, smem] + [vmem] * 3,
        out_specs=(vmem,) * 2,
        compiler_params=params,
        cost_estimate=pl.CostEstimate(flops=3000000000, bytes_accessed=10**6, transcendentals=0),
        name="pivots",
    )(pole_shift, which, first, *tails)
    w, *u = pl.pallas_call(
        solve_kernel,
        out_shape=(
            jax.ShapeDtypeStruct((depth, width), BF16),
            jax.ShapeDtypeStruct((2 * SN, width), BF16),
            jax.ShapeDtypeStruct((2 * SN, width), BF16),
        ),
        in_specs=[smem] + [vmem] * 3,
        out_specs=(vmem,) * 3,
        compiler_params=params,
        name="solve",
    )(which, cross_rows, solve, special)

    offset = my_row // 2

    anywhere = pl.BlockSpec(memory_space=pl.ANY)

    def pick(index, *arrays):
        return pl.pallas_call(
            pick_kernel,
            out_shape=jax.ShapeDtypeStruct(arrays[0].shape, arrays[0].dtype),
            in_specs=[smem] + [anywhere] * 3,
            out_specs=vmem,
            scratch_shapes=[pltpu.SemaphoreType.DMA],
            compiler_params=params,
            name="pick",
        )(index.astype(jnp.int32)[None], *arrays)

    def along_y(array, hops):
        return lax.ppermute(
            array,
            both,
            [(device(2 * start, c), device(2 * end, c)) for c in columns for start, end in hops],
        )

    up, down = along_y(w, [(0, 3)]), along_y(w, [(0, 6)])
    w = pick(jnp.where(same_core, jnp.where(offset == 3, 1, jnp.where(offset == 6, 2, 0)), 0), w, up, down)
    up, down = along_y(w, [(0, 1), (3, 4)]), along_y(w, [(0, 7), (3, 2), (6, 5)])
    base = pl.pallas_call(
        assemble_kernel,
        out_shape=jax.ShapeDtypeStruct((2, height, width), F32),
        in_specs=[smem, smem, smem] + [vmem] * 2,
        out_specs=vmem,
        compiler_params=params,
        name="assemble",
    )(pole_shift, which, local_pattern, place[:, None], main)
    early = [
        lax.ppermute(u[i - 1], both, [(device(0, c), device(i, c)) for c in columns])
        for i in range(1, STEPS)
    ]
    up, down, early = lax.optimization_barrier((up, down, early))
    near = (offset == 1) | (offset == 4)
    kept = (offset == 0) | (offset == 3) | (offset == 6)
    w = jnp.where(kept, w, jnp.where(near, up, down))
    other = lax.ppermute(
        w,
        both,
        [(device(row, c), device(row + 1, c)) for c in columns for row in range(0, grid_rows, 2)],
    )
    return pl.pallas_call(
        update_kernel,
        out_shape=jax.ShapeDtypeStruct((2, height, width), F32),
        in_specs=[smem, smem] + [vmem] * 6,
        out_specs=pl.BlockSpec(memory_space=pl.ANY),
        scratch_shapes=[
            pltpu.VMEM((2, height, width), F32),
            pltpu.SemaphoreType.DMA((row_slots, 2)),
        ],
        compiler_params=params,
        name="update",
    )(pole_shift, which, base, panel, w, other, *early)


def solution(mesh):
    return jax.shard_map(
        body,
        mesh=mesh,
        in_specs=(P(("prow", "pcol"), None), P(("prow", "pcol"), None), P("pole"), P("prow"), P()),
        out_specs=P("pole", "prow", "pcol"),
        check_vma=False,
    )
```

```python
import functools

import jax
import jax.numpy as jnp
from jax import lax
from jax.experimental import pallas as pl
from jax.experimental.pallas import tpu as pltpu
from jax.sharding import PartitionSpec as P

SN = 128
STEPS = 3
NSI = 4
NBW = 96
CB = 2
N_Z = 12
N_X = 4
F32 = jnp.float32
BF16 = jnp.bfloat16


def embed(block):
    real, imag = block[:, :SN], block[:, SN:]
    return jnp.concatenate([block, jnp.concatenate([-imag, real], axis=1)], axis=0)


def times(left, right):
    return jnp.dot(left.astype(BF16), embed(right.astype(BF16)), preferred_element_type=F32)


def invert_pivot(pivot):
    row = lax.broadcasted_iota(jnp.int32, (SN, SN), 0)
    col = lax.broadcasted_iota(jnp.int32, (SN, SN), 1)
    eye = (row == col).astype(F32)
    real, imag = pivot[:, :SN], pivot[:, SN:]
    diag_real = jnp.sum(real * eye, axis=0, keepdims=True)
    diag_imag = jnp.sum(imag * eye, axis=0, keepdims=True)
    modulus = diag_real * diag_real + diag_imag * diag_imag
    inv_real, inv_imag = diag_real / modulus, -diag_imag / modulus
    res_real = eye - (real * inv_real - imag * inv_imag)
    res_imag = -(real * inv_imag + imag * inv_real)
    scale_real = jnp.sum(eye * inv_real, axis=1, keepdims=True)
    scale_imag = jnp.sum(eye * inv_imag, axis=1, keepdims=True)
    plus_real = eye + res_real
    approx = jnp.concatenate(
        [
            scale_real * plus_real - scale_imag * res_imag,
            scale_real * res_imag + scale_imag * plus_real,
        ],
        axis=1,
    )
    residue = jnp.concatenate([res_real, res_imag], axis=1)
    power = times(residue, residue)
    for sweep in range(NSI - 2):
        both = times(jnp.concatenate([approx, power], axis=0), power)
        approx, power = approx + both[:SN], both[SN:]
    return approx + times(approx, power)


def spread_kernel(ham_ref, over_ref, out_ref, own_ref, sems):
    stride = ham_ref.shape[1] // (NBW // CB)
    copies = []
    for k, ref in enumerate((ham_ref, over_ref)):
        for t in range(STEPS):
            piece = k * STEPS + t
            copies.append(
                pltpu.make_async_copy(
                    ref.at[:, t * stride : t * stride + SN],
                    own_ref.at[:, piece * SN : (piece + 1) * SN],
                    sems.at[piece],
                )
            )
    for copy in copies:
        copy.start()
    for copy in copies:
        copy.wait()
    for receiver in range(out_ref.shape[0]):
        out_ref[receiver] = own_ref[...]


def pack_kernel(ham_ref, over_ref, out_ref):
    band, width = out_ref.shape[1] // 2, out_ref.shape[2]
    for col in range(out_ref.shape[0]):
        cols = slice(col * width, (col + 1) * width)
        out_ref[col, :band] = ham_ref[:, cols]
        out_ref[col, band:] = over_ref[:, cols]


def pick_rows(place, chunks):
    start, total = 0, None
    for chunk in chunks:
        length = chunk.shape[0]
        pick = (
            place - start == lax.broadcasted_iota(jnp.int32, (SN, length), 1)
        ).astype(BF16)
        part = jnp.dot(pick, chunk[...], preferred_element_type=F32)
        total = part if total is None else total + part
        start += length
    return total


def store_masked(out_ref, rows, got, mask_ref, slot):
    for part in range(2 * STEPS):
        cols = slice(part * SN, (part + 1) * SN)
        out_ref[rows, cols] = (got[:, cols] * mask_ref[slot, part % STEPS]).astype(BF16)


def early_kernel(slot_ref, mask_ref, place_ref, *refs):
    chunks, (own_ref, tail1_ref, tail2_ref, cross_ref) = refs[:-4], refs[-4:]

    @pl.when(slot_ref[0] >= 0)
    def _():
        got = pick_rows(place_ref[:SN, :], chunks)
        store_masked(own_ref, slice(0, SN), got, mask_ref, 0)
        for first, out_ref in ((1, tail1_ref), (2, tail2_ref)):
            length = (STEPS - first) * SN
            for part in range(2):
                start = (part * STEPS + first) * SN
                out_ref[:, part * length : (part + 1) * length] = own_ref[
                    :, start : start + length
                ]

    @pl.when(slot_ref[1] >= 0)
    def _():
        for block in range(cross_ref.shape[0] // SN):
            slot = slot_ref[1 + block]
            place = place_ref[pl.ds(pl.multiple_of(slot * SN, SN), SN), :]
            rows = slice(block * SN, (block + 1) * SN)
            store_masked(cross_ref, rows, pick_rows(place, chunks), mask_ref, slot)


def panel_kernel(mask_ref, place_ref, *refs):
    chunks, out_ref = refs[:-1], refs[-1]
    for slot in range(out_ref.shape[0] // SN):
        rows = slice(slot * SN, (slot + 1) * SN)
        store_masked(out_ref, rows, pick_rows(place_ref[rows, :], chunks), mask_ref, slot)


def for_raw_rows(z_real, z_imag, blocks):
    real, imag = blocks
    return z_imag * imag - z_real * real, -z_real * imag - z_imag * real


def shifted(shift_ref, ref, step, count):
    ham = ref[:, step * SN : (step + 1) * SN].astype(F32)
    over = ref[:, (count + step) * SN : (count + step + 1) * SN].astype(F32)
    return jnp.concatenate([ham - shift_ref[0] * over, -shift_ref[1] * over], axis=1)


def flip(block):
    return jnp.concatenate([block[:, :SN].T, block[:, SN:].T], axis=1)


def stacked(lefts, right):
    product = times(jnp.concatenate(lefts, axis=0), right)
    return [product[i * SN : (i + 1) * SN] for i in range(len(lefts))]


def first_pivot_kernel(shift_ref, own_ref, out_ref):
    a00, a01, a02 = [shifted(shift_ref, own_ref, s, STEPS) for s in range(STEPS)]
    x0 = invert_pivot(a00)
    f10, f20 = stacked([flip(a01), flip(a02)], x0)
    out_ref[0], out_ref[1], out_ref[2] = x0, f10, f20
    out_ref[3] = times(f10, a01)
    out_ref[4], out_ref[5] = stacked([f10, f20], a02)


def pivot_kernel(shift_ref, which_ref, first_ref, a1_ref, a2_ref, solve_ref, special_ref):
    z_real, z_imag = shift_ref[0], shift_ref[1]
    my_col = which_ref[0]
    x0, f10, f20 = first_ref[0], first_ref[1], first_ref[2]
    a11 = shifted(shift_ref, a1_ref, 0, 2) - first_ref[3]
    a12 = shifted(shift_ref, a1_ref, 1, 2) - first_ref[4]
    a22 = shifted(shift_ref, a2_ref, 0, 1) - first_ref[5]
    x1 = invert_pivot(a11)
    f21 = times(flip(a12), x1)
    x2 = invert_pivot(a22 - times(f21, a12))
    k01, k12 = -flip(f10), -flip(f21)
    k02 = times(k01, k12) - flip(f20)
    h01 = times(k01, x1)
    h12, h02 = stacked([k12, k02], x2)
    by_f10 = stacked([f21, h01, x1], f10)
    back = by_f10[0] - f20
    by_back = stacked([h02, x2], back)
    by_f21 = stacked([h12, h02, x2], f21)
    m20 = by_back[1]
    solve = [
        [x0 - by_f10[1] + by_back[0], h01 - by_f21[1], h02],
        [times(k12, m20) - by_f10[2], x1 - by_f21[0], h12],
        [m20, -by_f21[2], x2],
    ]
    zero = jnp.zeros((SN, 2 * SN), F32)
    half = STEPS * SN

    def store(row, stride, parts):
        real = jnp.concatenate([p[:, :SN] for p in parts], axis=1)
        imag = jnp.concatenate([p[:, SN:] for p in parts], axis=1)
        over_real, over_imag = for_raw_rows(z_real, z_imag, (real, imag))
        for offset, ham, over in ((0, real, over_real), (stride, imag, over_imag)):
            rows = slice(row + offset, row + offset + SN)
            solve_ref[rows, :half] = ham.astype(BF16)
            solve_ref[rows, half:] = over.astype(BF16)

    for t in range(STEPS):
        store(t * SN, half, solve[t])
    store(2 * half, SN, [f10, zero, zero])
    store(2 * half + 2 * SN, SN, [-back, f21, zero])
    upper = [[x0, h01, h02], [zero, x1, h12], [zero, zero, x2]]
    for s in range(STEPS):
        total = jnp.where(my_col == 0, upper[s][0], upper[s][1])
        total = jnp.where(my_col == 2, upper[s][2], total)
        special_ref[s * SN : (s + 1) * SN, :] = total[:, :SN].astype(BF16)
        special_ref[half + s * SN : half + (s + 1) * SN, :] = total[:, SN:].astype(BF16)
    for i, total in enumerate((f10, jnp.where(my_col == 0, f20, f21))):
        row = 2 * half + 2 * i * SN
        special_ref[row : row + SN, :] = total[:, :SN].astype(BF16)
        special_ref[row + SN : row + 2 * SN, :] = total[:, SN:].astype(BF16)


def solve_kernel(which_ref, cross_ref, solve_ref, special_ref, w_ref, u1_ref, u2_ref):
    my_col = which_ref[0]
    start = 0
    for out_ref, limit in ((w_ref, STEPS), (u1_ref, 1), (u2_ref, 2)):
        rows = slice(start, start + out_ref.shape[0])
        got = lax.dot_general(
            solve_ref[rows, :],
            cross_ref[...],
            (((1,), (1,)), ((), ())),
            preferred_element_type=F32,
        ).astype(BF16)
        out_ref[:, SN:] = got[:, SN:]
        out_ref[:, :SN] = jnp.where(my_col < limit, special_ref[rows, :], got[:, :SN])
        start += out_ref.shape[0]


def is_factor(which_ref, slot, half):
    node = which_ref[1] + which_ref[2] * slot
    return (which_ref[0] < STEPS) & (node > which_ref[0]) if half == 0 else None


def assemble_kernel(shift_ref, which_ref, mask_ref, place_ref, main_ref, out_ref):
    z_real, z_imag = shift_ref[0], shift_ref[1]
    height, width = out_ref.shape[1], out_ref.shape[2]
    band = main_ref.shape[1] // 2
    ham_raw = main_ref[:, :band, :].reshape(height, width)
    over_raw = main_ref[:, band:, :].reshape(height, width)
    for slot in range(height // SN):
        rows = slice(slot * SN, (slot + 1) * SN)
        place = place_ref[rows, :]
        ham = pick_rows(place, [ham_raw])
        over = pick_rows(place, [over_raw])
        real, imag = ham - z_real * over, -z_imag * over
        for half in range(width // SN):
            cols = slice(half * SN, (half + 1) * SN)
            keep = mask_ref[slot, half]
            factor = is_factor(which_ref, slot, half)
            if factor is not None:
                keep = jnp.where(factor, 0.0, keep)
            out_ref[0, rows, cols] = real[:, cols] * keep
            out_ref[1, rows, cols] = imag[:, cols] * keep


def update_kernel(
    shift_ref,
    which_ref,
    base_ref,
    panel_ref,
    w_ref,
    w_other_ref,
    u1_ref,
    u2_ref,
    out_ref,
    done_ref,
    sems,
):
    z_real, z_imag = shift_ref[0], shift_ref[1]
    my_row, own = which_ref[1], which_ref[3] > 0
    height, width = out_ref.shape[1], out_ref.shape[2]
    w = jnp.where(own, w_ref[...], w_other_ref[...])
    half = w.shape[0] // 2
    over_real, over_imag = for_raw_rows(
        z_real, z_imag, (w[:half].astype(F32), w[half:].astype(F32))
    )
    w_all = jnp.concatenate(
        [
            jnp.concatenate([w[:half], w[half:]], axis=1),
            jnp.concatenate([over_real, over_imag], axis=1).astype(BF16),
        ],
        axis=0,
    )
    copies = []
    for slot in range(height // SN):
        rows = slice(slot * SN, (slot + 1) * SN)
        change = jnp.dot(panel_ref[rows, :], w_all, preferred_element_type=F32)
        for part in range(2):
            part_change = change[:, part * width : (part + 1) * width]
            if slot == 0:
                block = slice(part * SN, (part + 1) * SN)
                later = jnp.where(my_row == 1, u1_ref[block, :].astype(F32), part_change)
                later = jnp.where(my_row == 2, u2_ref[block, :].astype(F32), later)
                part_change = jnp.where(my_row == 0, 0.0, later)
            for piece in range(width // SN):
                cols = slice(piece * SN, (piece + 1) * SN)
                factor = is_factor(which_ref, slot, piece)
                sign = -1.0 if factor is None else jnp.where(factor, 1.0, -1.0)
                done_ref[part, rows, cols] = (
                    base_ref[part, rows, cols] + part_change[:, cols] * sign
                )
            copy = pltpu.make_async_copy(
                done_ref.at[part, rows], out_ref.at[part, rows], sems.at[slot, part]
            )
            copy.start()
            copies.append(copy)
    for copy in copies:
        copy.wait()


def structure(parent, node_count):
    node_index = jnp.arange(node_count, dtype=jnp.int32)
    reached = (parent[:, None] == node_index[None, :]).astype(BF16)
    for level_index in range(node_count.bit_length()):
        more = jnp.dot(reached, reached, preferred_element_type=F32)
        reached = ((reached.astype(F32) + more) > 0.5).astype(BF16)
    diagonal_ones = (node_index[:, None] == node_index[None, :]).astype(F32)
    return jnp.minimum(diagonal_ones + reached.astype(F32) + reached.T.astype(F32), 1.0)


def body(hamiltonian, margin, pole_shift, row_map, parent):
    grid_rows = lax.axis_size("prow")
    grid_cols = lax.axis_size("pcol")
    my_row = lax.axis_index("prow")
    my_col = lax.axis_index("pcol")
    node_count = parent.shape[0]
    band = hamiltonian.shape[0]
    height = band * grid_cols
    width = hamiltonian.shape[1] // grid_cols
    row_slots, col_slots = height // SN, width // SN

    smem = pl.BlockSpec(memory_space=pltpu.SMEM)
    vmem = pl.BlockSpec(memory_space=pltpu.VMEM)
    params = pltpu.CompilerParams(vmem_limit_bytes=20 * 1024 * 1024)
    full = pltpu.CompilerParams(vmem_limit_bytes=56 * 1024 * 1024)
    both = ("prow", "pcol")

    def device(row, col):
        return row * grid_cols + col

    hbm = pl.BlockSpec(memory_space=pltpu.HBM)
    pieces = 2 * STEPS
    copies = pl.pallas_call(
        spread_kernel,
        out_shape=jax.ShapeDtypeStruct((N_Z, band, pieces * SN), BF16),
        in_specs=[hbm, hbm],
        out_specs=vmem,
        scratch_shapes=[
            pltpu.VMEM((band, pieces * SN), BF16),
            pltpu.SemaphoreType.DMA((pieces,)),
        ],
        compiler_params=full,
        name="spread",
    )(hamiltonian, margin)
    along_z = [[z * N_X + x for z in range(N_Z)] for x in range(N_X)]
    held_rows = N_Z * band
    mine = lax.all_to_all(copies, "pcol", 0, 0, axis_index_groups=along_z).reshape(held_rows, -1)

    packed = pl.pallas_call(
        pack_kernel,
        out_shape=jax.ShapeDtypeStruct((grid_cols, 2 * band, width), BF16),
        in_specs=[vmem, vmem],
        out_specs=vmem,
        compiler_params=full,
        name="pack",
    )(hamiltonian, margin)
    packed, mine = lax.optimization_barrier((packed, mine))

    def shift_x(array, by):
        return lax.ppermute(
            array, "pcol", [(c, c - c % N_X + (c % N_X + by) % N_X) for c in range(grid_cols)]
        )

    below, above = shift_x(mine, 1), shift_x(mine, -1)
    far_first = shift_x(below[: held_rows // 2], 1)
    far_last = shift_x(above[held_rows // 2 :], -1)
    chunks = [mine, above, far_first, far_last, below]
    main = lax.all_to_all(packed, "pcol", 0, 0)
    pattern = structure(parent, node_count)
    row_nodes = jnp.arange(row_slots, dtype=jnp.int32) * grid_rows + my_row
    col_nodes = jnp.arange(col_slots, dtype=jnp.int32) * grid_cols + my_col
    all_nodes = jnp.arange(node_count, dtype=jnp.int32)
    pick_rows = (row_nodes[:, None] == all_nodes[None, :]).astype(F32)
    pick_cols = (col_nodes[:, None] == all_nodes[None, :]).astype(F32)
    row_pattern = jnp.dot(pick_rows, pattern)
    local_pattern = jnp.dot(row_pattern, pick_cols.T)
    panel_pattern = row_pattern[:, :STEPS]

    place = row_map - my_row * height
    source, inner = place // band, place % band
    distance = (source % N_X - my_col % N_X) % N_X
    panel_place = distance * held_rows + source // N_X * band + inner
    same_core = my_row % 2 == 0
    which = jnp.stack(
        [my_col, my_row, jnp.int32(grid_rows), same_core.astype(jnp.int32)]
    ).astype(jnp.int32)
    first_slot = my_col // grid_rows
    slots = jnp.stack([first_slot, first_slot + grid_cols // grid_rows]).astype(jnp.int32)

    depth = 2 * STEPS * SN
    panel_place = panel_place[:, None]
    columns = range(grid_cols)
    wanted = jnp.concatenate(
        [
            jnp.where(my_row < STEPS, 0, -1)[None].astype(jnp.int32),
            jnp.where(my_row == my_col % grid_rows, slots, -1),
        ]
    )
    own_rows, tail1, tail2, cross_rows = pl.pallas_call(
        early_kernel,
        out_shape=tuple(
            jax.ShapeDtypeStruct(shape, BF16)
            for shape in ((SN, depth), (SN, 4 * SN), (SN, 2 * SN), (width, depth))
        ),
        in_specs=[smem, smem, vmem] + [vmem] * len(chunks),
        out_specs=(vmem,) * 4,
        compiler_params=params,
        name="early_rows",
    )(wanted, panel_pattern, panel_place, *chunks)
    tails = [
        lax.ppermute(tail, both, [(device(t, c), device(0, c)) for c in columns])
        for t, tail in ((1, tail1), (2, tail2))
    ]
    cross_rows = lax.ppermute(
        cross_rows, both, [(device(c % grid_rows, c), device(0, c)) for c in columns]
    )
    first = pl.pallas_call(
        first_pivot_kernel,
        out_shape=jax.ShapeDtypeStruct((6, SN, 2 * SN), F32),
        in_specs=[smem, vmem],
        out_specs=vmem,
        compiler_params=params,
        name="first_pivot",
    )(pole_shift, own_rows)
    panel = pl.pallas_call(
        panel_kernel,
        out_shape=jax.ShapeDtypeStruct((height, 2 * STEPS * SN), BF16),
        in_specs=[smem, vmem] + [vmem] * len(chunks),
        out_specs=vmem,
        compiler_params=params,
        name="panel_rows",
    )(panel_pattern, panel_place, *chunks)

    *tails, panel, first = lax.optimization_barrier((*tails, panel, first))
    solve_height = depth + 2 * (STEPS - 1) * SN
    solve, special = pl.pallas_call(
        pivot_kernel,
        out_shape=(
            jax.ShapeDtypeStruct((solve_height, depth), BF16),
            jax.ShapeDtypeStruct((solve_height, SN), BF16),
        ),
        in_specs=[smem, smem] + [vmem] * 3,
        out_specs=(vmem,) * 2,
        compiler_params=params,
        cost_estimate=pl.CostEstimate(flops=3000000000, bytes_accessed=10**6, transcendentals=0),
        name="pivots",
    )(pole_shift, which, first, *tails)
    w, *u = pl.pallas_call(
        solve_kernel,
        out_shape=(
            jax.ShapeDtypeStruct((depth, width), BF16),
            jax.ShapeDtypeStruct((2 * SN, width), BF16),
            jax.ShapeDtypeStruct((2 * SN, width), BF16),
        ),
        in_specs=[smem] + [vmem] * 3,
        out_specs=(vmem,) * 3,
        compiler_params=params,
        name="solve",
    )(which, cross_rows, solve, special)

    offset = my_row // 2

    def along_y(array, hops):
        return lax.ppermute(
            array,
            both,
            [(device(2 * start, c), device(2 * end, c)) for c in columns for start, end in hops],
        )

    up, down = along_y(w, [(0, 3)]), along_y(w, [(0, 6)])
    w = jnp.where((offset == 3) & same_core, up, jnp.where((offset == 6) & same_core, down, w))
    up, down = along_y(w, [(0, 1), (3, 4)]), along_y(w, [(0, 7), (3, 2), (6, 5)])
    base = pl.pallas_call(
        assemble_kernel,
        out_shape=jax.ShapeDtypeStruct((2, height, width), F32),
        in_specs=[smem, smem, smem] + [vmem] * 2,
        out_specs=vmem,
        compiler_params=params,
        name="assemble",
    )(pole_shift, which, local_pattern, place[:, None], main)
    early = [
        lax.ppermute(u[i - 1], both, [(device(0, c), device(i, c)) for c in columns])
        for i in range(1, STEPS)
    ]
    up, down, early = lax.optimization_barrier((up, down, early))
    near = (offset == 1) | (offset == 4)
    kept = (offset == 0) | (offset == 3) | (offset == 6)
    w = jnp.where(kept, w, jnp.where(near, up, down))
    other = lax.ppermute(
        w,
        both,
        [(device(row, c), device(row + 1, c)) for c in columns for row in range(0, grid_rows, 2)],
    )
    return pl.pallas_call(
        update_kernel,
        out_shape=jax.ShapeDtypeStruct((2, height, width), F32),
        in_specs=[smem, smem] + [vmem] * 6,
        out_specs=pl.BlockSpec(memory_space=pl.ANY),
        scratch_shapes=[
            pltpu.VMEM((2, height, width), F32),
            pltpu.SemaphoreType.DMA((row_slots, 2)),
        ],
        compiler_params=params,
        name="update",
    )(pole_shift, which, base, panel, w, other, *early)


def solution(mesh):
    return jax.shard_map(
        body,
        mesh=mesh,
        in_specs=(P(("prow", "pcol"), None), P(("prow", "pcol"), None), P("pole"), P("prow"), P()),
        out_specs=P("pole", "prow", "pcol"),
        check_vma=False,
    )
```
